128 devices in a mesh: ty: 8 (over x, core), tx: 16 (over z, y).
Axes of the slice: x: 4, y: 4, z: 4, core: 2. Of those that a mesh axis runs over, the one named last changes fastest.
Arguments:
- features: bfloat16 [256, 512, 512], P('ty', 'tx'), may hold values from -6 to 6
- block_reduce: bfloat16 [2, 512, 128], replicated, may hold values from -0.375 to 0.375
- block_spatial: bfloat16 [2, 9, 128, 128], replicated, may hold values from -0.25 to 0.25
- block_expand: bfloat16 [2, 128, 512], replicated, may hold values from -0.5 to 0.5
- mask_first: bfloat16 [9, 512, 256], replicated, may hold values from -0.125 to 0.125
- mask_rest: bfloat16 [3, 9, 256, 256], replicated, may hold values from -0.1875 to 0.1875
- mask_logit: bfloat16 [256], replicated, may hold values from -0.5 to 0.5
- box_reduce: bfloat16 [512, 128], replicated, may hold values from -0.25 to 0.25
- box_hidden: bfloat16 [6272, 1024], replicated, may hold values from -0.109375 to 0.109375
- box_second: bfloat16 [1024, 1024], replicated, may hold values from -0.25 to 0.25
- box_predict: bfloat16 [1024, 5], replicated, may hold values from -0.25 to 0.25
- roi_anchor: int32 [8, 16, 32, 2], P('ty', 'tx'), may hold values from 0 to 18
- roi_dest: int32 [8, 16, 32], P('ty', 'tx'), may hold values from -1 to 15, as said below
- roi_slot: int32 [8, 16, 32], P('ty', 'tx'), may hold values from -1 to 15, as said below
Outputs:
- section_features: bfloat16 [256, 512, 512], P('ty', 'tx')
- mask_logits: float32 [8, 16, 32, 196], P('ty', 'tx')
- box_scores: float32 [8, 16, 32, 5], P('ty', 'tx')
The draws below stay inside these ranges and needn't reach their ends.
Inputs may be any that keep to these rules, and one draw needn't show every extreme that they name: `roi_dest`: -1 marks an unused slot; used slots of a tile come first; in each row of tiles every head column receives exactly 16 ROIs; used slots of one tile with the same value lie a multiple of 16 positions apart. -1 exactly where roi_dest is -1; within one row of tiles no two used slots share both roi_dest and roi_slot.
All inputs are finite; a program needn't handle non-finite values.
Results may differ from the reference program's by a relative error of at most 0.033.
Values may be sent and summed in bfloat16 or wider, within the bound.
No kernel may reach another device: no remote copies, remote signals or barrier semaphores. Data moves between devices by JAX's collectives and lax.ppermute only.
A program may use at most 128 MiB of HBM per device.

```python
import jax
import jax.numpy as jnp
from jax import lax

CH = 512
INNER = 128
MASK_CH = 256
BOX_CH = 128
FC = 1024
CROP = 14
ROWS = 32
COLS = 32
HEAD = 16
ROI_MAX = 32
TILES_Y = 8
TILES_X = 16


def assign_lists(key):
    perm_key, pair_key, turn_key = jax.random.split(jax.random.fold_in(key, 7), 3)
    row_keys = jax.random.split(perm_key, TILES_Y)
    order = jax.vmap(lambda row_key: jax.random.permutation(row_key, TILES_X))(row_keys)
    amount = jax.random.randint(pair_key, (TILES_Y, TILES_X // 2), 0, HEAD + 1)
    amount = jnp.where(jnp.arange(TILES_X // 2)[None, :] == 0, HEAD, amount)
    paired = jnp.stack([HEAD + amount, HEAD - amount], axis=2).reshape(TILES_Y, TILES_X)
    counts = jnp.take_along_axis(paired, jnp.argsort(order, axis=1), axis=1)
    starts = jnp.cumsum(counts, axis=1) - counts
    turn = jax.random.randint(turn_key, (TILES_Y, 1, 1), 0, TILES_X)
    lane_index = jnp.arange(ROI_MAX)[None, None, :]
    ranking = starts[:, :, None] + lane_index
    is_live = lane_index < counts[:, :, None]
    destination = jnp.where(is_live, (ranking + turn) % TILES_X, -1)
    head_slot = jnp.where(is_live, ranking // TILES_X, -1)
    return (destination.astype(jnp.int32), head_slot.astype(jnp.int32))


def draw_roi_dest(key, part):
    return assign_lists(key)[0]


def draw_roi_slot(key, part):
    return assign_lists(key)[1]


def with_ends(entries, key, smallest, top_value):
    longest = entries.shape.index(max(entries.shape))
    spots = []
    for shift in (0, 1):
        where = [jax.random.randint(jax.random.fold_in(key, axis), (), 0, length) for axis, length in enumerate(entries.shape)]
        where[longest] = (where[longest] + shift) % entries.shape[longest]
        spots.append(tuple(where))
    return entries.at[spots[0]].set(smallest).at[spots[1]].set(top_value)


def shard_levels(rng, dims, cuts, smallest, high):
    def one(axis_at, parts):
        draws = jax.random.uniform(jax.random.fold_in(jax.random.fold_in(rng, 6), axis_at), (parts,), jnp.float32, smallest / len(cuts), high / len(cuts))
        return jnp.repeat(jnp.exp(draws), dims[axis_at] // parts).reshape((-1,) + (1,) * (len(dims) - axis_at - 1))

    factor_of = one(*cuts[0])
    for cut in cuts[1:]:
        factor_of = factor_of * one(*cut)
    return factor_of


def noise(own_key, shape, scale, limit, cuts=(), held_as=jnp.bfloat16):
    drawn = jax.random.normal(own_key, shape, jnp.float32) * scale
    if len(cuts) > 0:
        drawn = shard_levels(own_key, shape, cuts, -0.22, 0.18) * drawn
    return jnp.clip(drawn, min=-limit, max=limit).astype(held_as)


def setup_inputs(seed: int = 0) -> dict:
    keys = jax.random.split(jax.random.key(seed), 15)
    features = noise(keys[0], (TILES_Y * ROWS, TILES_X * COLS, CH), 1.0, 6.0, ((0, 8), (1, 16)))
    block_reduce = noise(keys[1], (2, CH, INNER), (CH // 2) ** -0.5, 0.375)
    block_spatial = noise(keys[2], (2, 9, INNER, INNER), (9 * INNER // 2) ** -0.5, 0.25)
    block_expand = noise(keys[3], (2, INNER, CH), INNER ** -0.5, 0.5)
    mask_first = noise(keys[4], (9, CH, MASK_CH), (9 * CH // 2) ** -0.5, 0.125)
    mask_rest = noise(keys[5], (3, 9, MASK_CH, MASK_CH), (9 * MASK_CH // 2) ** -0.5, 0.1875)
    mask_logit = noise(keys[6], (MASK_CH,), (MASK_CH // 2) ** -0.5, 0.5)
    box_reduce = noise(keys[7], (CH, BOX_CH), CH ** -0.5, 0.25)
    box_hidden = noise(keys[8], ((CROP // 2) ** 2 * BOX_CH, FC), ((CROP // 2) ** 2 * BOX_CH // 2) ** -0.5, 0.109375)
    box_second = noise(keys[9], (FC, FC), (FC // 2) ** -0.5, 0.25)
    box_predict = noise(keys[10], (FC, 5), (FC // 2) ** -0.5, 0.25)
    roi_anchor = with_ends(jax.random.randint(keys[11], (TILES_Y, TILES_X, ROI_MAX, 2), 0, min(ROWS, COLS) - CROP + 1), jax.random.fold_in(keys[11], 1), 0, min(ROWS, COLS) - CROP).astype(jnp.int32)
    roi_dest = draw_roi_dest(jax.random.fold_in(keys[14], 71), 0)
    roi_slot = draw_roi_slot(jax.random.fold_in(keys[14], 71), 0)
    return {"features": features, "block_reduce": block_reduce, "block_spatial": block_spatial, "block_expand": block_expand, "mask_first": mask_first, "mask_rest": mask_rest, "mask_logit": mask_logit, "box_reduce": box_reduce, "box_hidden": box_hidden, "box_second": box_second, "box_predict": box_predict, "roi_anchor": roi_anchor, "roi_dest": roi_dest, "roi_slot": roi_slot}


def conv_three(padded, weights, out_rows, out_cols):
    lead_shape = padded.shape[:-3]
    rows_in, cols_in, chans = padded.shape[-3:]
    width = ((cols_in + 7) // 8) * 8
    pad_spec = [(0, 0)] * len(lead_shape) + [(0, 0), (0, width - cols_in), (0, 0)]
    flat_rows = jnp.pad(padded, pad_spec).reshape(-1, chans)
    row_total = flat_rows.shape[0]
    flat_rows = jnp.pad(flat_rows, ((0, 2 * width + 2), (0, 0)))
    summed = None
    for offset in range(9):
        start_row = (offset // 3) * width + offset % 3
        window = flat_rows[start_row:start_row + row_total]
        partial_sum = jnp.dot(window, weights[offset], preferred_element_type=jnp.float32)
        summed = partial_sum if summed is None else summed + partial_sum
    summed = summed.reshape(lead_shape + (rows_in, width, weights.shape[-1]))
    return summed[..., :out_rows, :out_cols, :]


def pad_crop(crop_batch):
    return jnp.pad(crop_batch, ((0, 0), (1, 1), (1, 1), (0, 0)))


def mask_stem(crops, mask_first, box_reduce):
    number, crop_side = crops.shape[0], crops.shape[1]
    mask_one = jax.nn.relu(conv_three(pad_crop(crops), mask_first, crop_side, crop_side)).astype(jnp.bfloat16)
    reduced = jnp.dot(crops.reshape(-1, crops.shape[-1]), box_reduce, preferred_element_type=jnp.float32)
    half_side = crop_side // 2
    pooled = reduced.reshape(number, half_side, 2, half_side, 2, -1).mean(axis=(2, 4))
    return mask_one, pooled.astype(jnp.bfloat16).reshape(number, -1)


def finish(mask_one, box_input, mask_rest, mask_logit, box_hidden, box_second, box_predict):
    number, crop_side = mask_one.shape[0], mask_one.shape[1]
    mask_layer = mask_one
    for section_index in range(mask_rest.shape[0]):
        mask_layer = jax.nn.relu(conv_three(pad_crop(mask_layer), mask_rest[section_index], crop_side, crop_side)).astype(jnp.bfloat16)
    logits = jnp.dot(mask_layer.reshape(-1, mask_layer.shape[-1]), mask_logit[:, None], preferred_element_type=jnp.float32)
    logits = logits.reshape(number, crop_side * crop_side)
    box_first = jax.nn.relu(jnp.dot(box_input, box_hidden, preferred_element_type=jnp.float32)).astype(jnp.bfloat16)
    box_next = jax.nn.relu(jnp.dot(box_first, box_second, preferred_element_type=jnp.float32)).astype(jnp.bfloat16)
    scores = jnp.dot(box_next, box_predict, preferred_element_type=jnp.float32)
    return logits, scores


def block_step(feature_map, reduce_w, spatial_w, expand_w):
    map_rows, map_cols, chans = feature_map.shape
    inner_map = jax.nn.relu(jnp.dot(feature_map.reshape(-1, chans), reduce_w, preferred_element_type=jnp.float32))
    inner_map = inner_map.astype(jnp.bfloat16).reshape(map_rows, map_cols, -1)
    padded = jnp.pad(inner_map, ((1, 1), (1, 1), (0, 0)))
    spatial = jax.nn.relu(conv_three(padded, spatial_w, map_rows, map_cols)).astype(jnp.bfloat16)
    branch = jnp.dot(spatial.reshape(-1, spatial.shape[-1]), expand_w, preferred_element_type=jnp.float32)
    return jax.nn.relu(feature_map.astype(jnp.float32) + branch.reshape(map_rows, map_cols, chans)).astype(jnp.bfloat16)


def reference(features, block_reduce, block_spatial, block_expand, mask_first, mask_rest, mask_logit, box_reduce, box_hidden, box_second, box_predict, roi_anchor, roi_dest, roi_slot):
    feature_map = features
    for section_index in range(2):
        feature_map = block_step(feature_map, block_reduce[section_index], block_spatial[section_index], block_expand[section_index])
    tile_grid = feature_map.reshape(TILES_Y, ROWS, TILES_X, COLS, CH).transpose(0, 2, 1, 3, 4)

    def cut_crop(tile, anchor):
        start_list = (anchor[0].astype(jnp.int32), anchor[1].astype(jnp.int32), jnp.zeros((), jnp.int32))
        return lax.dynamic_slice(tile, start_list, (CROP, CROP, CH))

    crops = jax.vmap(jax.vmap(jax.vmap(cut_crop, in_axes=(None, 0))))(tile_grid, roi_anchor)
    place_keys = jnp.where(roi_dest >= 0, roi_dest * HEAD + roi_slot, -1).astype(jnp.int32)

    def row_heads(row_item):
        row_crops, row_keys = row_item
        flattened = row_crops.reshape(TILES_X * ROI_MAX, -1)
        places = jnp.arange(TILES_X * HEAD, dtype=jnp.int32)
        chooser = row_keys.reshape(-1)[None, :] == places[:, None]
        compact = jnp.dot(chooser.astype(jnp.bfloat16), flattened, preferred_element_type=jnp.float32)
        compact = compact.astype(jnp.bfloat16).reshape(TILES_X * HEAD, CROP, CROP, CH)
        mask_one, box_input = mask_stem(compact, mask_first, box_reduce)
        logits, scores = finish(mask_one, box_input, mask_rest, mask_logit, box_hidden, box_second, box_predict)
        spread_back = chooser.astype(jnp.float32).T
        return (jnp.dot(spread_back, logits, precision=lax.Precision.HIGHEST),
                jnp.dot(spread_back, scores, precision=lax.Precision.HIGHEST))

    logits, scores = lax.map(row_heads, (crops, place_keys))
    logits = logits.reshape(TILES_Y, TILES_X, ROI_MAX, CROP * CROP)
    scores = scores.reshape(TILES_Y, TILES_X, ROI_MAX, 5)
    return feature_map, logits, scores
```

```python
import jax
import jax.numpy as jnp
from jax import lax
from jax.experimental import pallas as pl
from jax.experimental.pallas import tpu as pltpu
from jax.sharding import PartitionSpec as P

CROP = 14
TILE = 32
WIDE = 48
TALL = 37
FLAT = TALL * WIDE
CH = 512
INNER = 128
MASK_CH = 256
BOX_CH = 128
FC = 1024
SLOTS = 32
WINDOW = 20
SPAN = WINDOW * TILE
BF = jnp.bfloat16
F32 = jnp.float32


def mm(a, b):
    return jnp.dot(a, b, preferred_element_type=F32)


def tile_kernel(
    feat, top, bottom, edge, w_red, w_spa, w_exp, w_first, w_rest, w_log, w_br, w_bh, w_bs, w_bp,
    base,
    sec, lg, sc,
    xe, inr, cat, xs, mv, taps, redf, avg, pick, pick_side, ma, mb, box_t,
    v_red, v_spa, v_exp, v_first, v_rest, v_br, v_bh, v_bs,
    sems,
):
    row_at = lax.axis_index("ty")
    col_at = lax.axis_index("tx")
    rows_of = lax.axis_size("ty")
    cols_of = lax.axis_size("tx")

    copies = [
        pltpu.make_async_copy(feat, xe.at[3:35, 0:TILE], sems.at[0]),
        pltpu.make_async_copy(top, xe.at[1:3, 0:TILE], sems.at[1]),
        pltpu.make_async_copy(bottom, xe.at[35:37, 0:TILE], sems.at[2]),
        pltpu.make_async_copy(edge, xe.at[0:TALL, TILE:WIDE], sems.at[3]),
        pltpu.make_async_copy(w_red, v_red, sems.at[4]),
        pltpu.make_async_copy(w_spa, v_spa, sems.at[5]),
        pltpu.make_async_copy(w_exp, v_exp, sems.at[6]),
        pltpu.make_async_copy(w_first, v_first, sems.at[7]),
        pltpu.make_async_copy(w_br, v_br, sems.at[8]),
        pltpu.make_async_copy(w_rest, v_rest, sems.at[9]),
        pltpu.make_async_copy(w_bh, v_bh, sems.at[10]),
        pltpu.make_async_copy(w_bs, v_bs, sems.at[11]),
    ]
    for copy in copies:
        copy.start()

    xe[0:1, 0:TILE, :] = jnp.zeros((1, TILE, CH), BF)
    inr[0:8, :] = jnp.zeros((8, INNER), F32)
    inr[8 + FLAT : 16 + FLAT, :] = jnp.zeros((8, INNER), F32)
    for j in range(3):
        xs[j, 0, :, :] = jnp.zeros((TILE, CH), BF)
        xs[j, TILE + 1, :, :] = jnp.zeros((TILE, CH), BF)
    for v in range(9):
        mv[v, TILE : TILE + 2, :, :] = jnp.zeros((2, TILE, MASK_CH), BF)
    redf[TILE * TILE : TILE * TILE + 40, :] = jnp.zeros((40, BOX_CH), F32)
    for ref in (ma, mb):
        ref[0, :, :, :] = jnp.zeros((16, SLOTS, MASK_CH), BF)
        ref[15, :, :, :] = jnp.zeros((16, SLOTS, MASK_CH), BF)
        ref[:, 0, :, :] = jnp.zeros((16, SLOTS, MASK_CH), BF)
        ref[:, 15, :, :] = jnp.zeros((16, SLOTS, MASK_CH), BF)

    at = base[...]
    lanes = lax.broadcasted_iota(jnp.int32, (SLOTS, SPAN), 1) - at
    for c in range(CROP):
        pick[c] = jnp.where(lanes == c, 1.0, 0.0).astype(BF)
    lanes = lax.broadcasted_iota(jnp.int32, (SLOTS, TILE * TILE), 1) - at
    for side, c in enumerate((0, CROP - 1)):
        for r in range(1, CROP - 1):
            pick_side[side, r - 1] = jnp.where(lanes == r * TILE + c, 1.0, 0.0).astype(BF)

    for copy in copies[:7]:
        copy.wait()

    for b in range(2):
        def reduce_rows(k, _):
            x = xe[pl.ds(k * 4, 4)].reshape(4 * WIDE, CH)
            h = jnp.maximum(mm(x, v_red[b]), 0.0)
            inr[pl.ds(pl.multiple_of(8 + k * 4 * WIDE, 8), 4 * WIDE), :] = h
            return 0

        lax.fori_loop(0, 9, reduce_rows, 0)
        x = xe[36:37].reshape(WIDE, CH)
        inr[8 + 36 * WIDE : 8 + FLAT, :] = jnp.maximum(mm(x, v_red[b]), 0.0)

        if b == 1:
            @pl.when(row_at == 0)
            def _():
                inr[8 + 2 * WIDE - 2 : 8 + 3 * WIDE - 2, :] = jnp.zeros((WIDE, INNER), F32)

            @pl.when(row_at == rows_of - 1)
            def _():
                inr[8 + 35 * WIDE - 2 : 8 + 36 * WIDE - 2, :] = jnp.zeros((WIDE, INNER), F32)

            @pl.when(col_at == 0)
            def _():
                inr[pl.ds(8 + WIDE - 1, TALL, stride=WIDE), :] = jnp.zeros((TALL, INNER), F32)

            @pl.when(col_at == cols_of - 1)
            def _():
                inr[pl.ds(8 + TILE, TALL, stride=WIDE), :] = jnp.zeros((TALL, INNER), F32)

        def shift_rows(k, _):
            here = pl.multiple_of(k * WIDE, 8)
            block = inr[pl.ds(here, WIDE + 16), :]
            for j in range(3):
                cat[k, :, j * INNER : (j + 1) * INNER] = block[7 + j : 7 + j + WIDE].astype(BF)
            return 0

        lax.fori_loop(0, TALL, shift_rows, 0)

        count = 5 if b == 0 else 4
        per = 7 if b == 0 else 8
        first = 1 if b == 0 else 3

        def spatial_rows(k, _):
            r = first + k * per
            lhs = jnp.concatenate([cat[pl.ds(r + i - 1, per)] for i in range(3)], axis=2)
            s = jnp.maximum(mm(lhs.reshape(per * WIDE, 9 * INNER), v_spa[b]), 0.0).astype(BF)
            y = mm(s, v_exp[b]) + xe[pl.ds(r, per)].reshape(per * WIDE, CH).astype(F32)
            y = jnp.maximum(y, 0.0).astype(BF)
            if b == 0:
                xe[pl.ds(r, per)] = y.reshape(per, WIDE, CH)
            else:
                xs[1, pl.ds(r - 2, per)] = y.reshape(per, WIDE, CH)[:, :TILE]
                wide = y.astype(F32)
                low = pltpu.roll(wide, 1, 0).reshape(per, WIDE, CH)[:, :TILE]
                high = pltpu.roll(wide, per * WIDE - 1, 0).reshape(per, WIDE, CH)[:, :TILE]
                xs[0, pl.ds(r - 2, per)] = low.astype(BF)
                xs[2, pl.ds(r - 2, per)] = high.astype(BF)
            return 0

        lax.fori_loop(0, count, spatial_rows, 0)

    out_copy = pltpu.make_async_copy(xs.at[1, 1 : TILE + 1], sec, sems.at[12])
    out_copy.start()
    copies[7].wait()
    copies[8].wait()

    def stem_rows(k, _):
        r = k * 8
        for i in range(3):
            for j in range(3):
                lhs = xs[j, pl.ds(r + i, 8)].reshape(8 * TILE, CH)
                taps[3 * i + j] = mm(lhs, v_first[3 * i + j])
        sums = []
        for i in range(3):
            t0, t1, t2 = taps[3 * i], taps[3 * i + 1], taps[3 * i + 2]
            right = t0 + t1
            sums.append((t1 + t2, right + t2, right))
        for cv in range(3):
            a0, a1, a2 = sums[0][cv], sums[1][cv], sums[2][cv]
            low = a0 + a1
            for rv, value in enumerate((a1 + a2, low + a2, low)):
                value = jnp.maximum(value, 0.0).astype(BF).reshape(8, TILE, MASK_CH)
                mv[3 * rv + cv, pl.ds(r, 8)] = value
        red = mm(xs[1, pl.ds(r + 1, 8)].reshape(8 * TILE, CH), v_br[...])
        redf[pl.ds(pl.multiple_of(r * TILE, 8), 8 * TILE), :] = red
        return 0

    lax.fori_loop(0, 4, stem_rows, 0)

    def average_rows(k, _):
        here = pl.multiple_of(k * 4 * TILE, 8)
        block = redf[pl.ds(here, 5 * TILE + 8), :]
        pair = block[: 5 * TILE] + block[1 : 5 * TILE + 1]
        quad = (pair[: 4 * TILE] + pair[TILE:]) * 0.25
        avg[pl.ds(k * 4, 4)] = quad.astype(BF).reshape(4, TILE, BOX_CH)
        return 0

    lax.fori_loop(0, 8, average_rows, 0)

    inside = CROP - 2

    def choose(picker, source):
        return mm(picker, source).astype(BF)

    def table(v, r):
        return mv[v, pl.ds(r, WINDOW)].reshape(SPAN, MASK_CH)

    def gather_row(r, _):
        got = choose(pick[1 : CROP - 1].reshape(inside * SLOTS, SPAN), table(4, r))
        ma[r + 1, 2 : CROP] = got.reshape(inside, SLOTS, MASK_CH)
        return 0

    lax.fori_loop(1, CROP - 1, gather_row, 0)
    last = CROP - 1
    for r, v in ((0, 1), (last, 7)):
        got = choose(pick[1:last].reshape(inside * SLOTS, SPAN), table(v, r))
        ma[r + 1, 2:CROP] = got.reshape(inside, SLOTS, MASK_CH)
        ma[r + 1, 1] = choose(pick[0], table(v - 1, r))
        ma[r + 1, CROP] = choose(pick[last], table(v + 1, r))
    for side, (c, v) in enumerate(((0, 3), (last, 5))):
        got = choose(
            pick_side[side].reshape(inside * SLOTS, TILE * TILE),
            mv[v, 0:TILE].reshape(TILE * TILE, MASK_CH),
        )
        ma[2:CROP, c + 1] = got.reshape(inside, SLOTS, MASK_CH)

    half = CROP // 2

    copies[9].wait()

    for layer in range(3):
        source, target = (ma, mb) if layer % 2 == 0 else (mb, ma)

        def conv_row(r, _):
            lhs = jnp.concatenate(
                [
                    source[r + i, j : j + CROP].reshape(CROP * SLOTS, MASK_CH)
                    for i in range(3)
                    for j in range(3)
                ],
                axis=1,
            )
            act = jnp.maximum(mm(lhs, v_rest[layer]), 0.0).astype(BF)
            if layer < 2:
                target[r + 1, 1 : CROP + 1] = act.reshape(CROP, SLOTS, MASK_CH)
            else:
                lg[r] = lax.dot_general(
                    w_log[...], act, (((1,), (1,)), ((), ())), preferred_element_type=F32
                )
            return 0

        lax.fori_loop(0, CROP, conv_row, 0)

    copies[10].wait()
    copies[11].wait()
    even = jnp.concatenate([pick[2 * u] for u in range(half)], axis=0)

    def box_row(t, total):
        got = choose(even, avg[pl.ds(2 * t, WINDOW)].reshape(SPAN, BOX_CH))
        for u in range(half):
            box_t[:, u * BOX_CH : (u + 1) * BOX_CH] = got[u * SLOTS : (u + 1) * SLOTS]
        part = v_bh[pl.ds(pl.multiple_of(t * half * BOX_CH, BOX_CH), half * BOX_CH), :]
        return total + mm(box_t[...], part)

    total = lax.fori_loop(0, half, box_row, jnp.zeros((SLOTS, FC), F32))
    first_box = jnp.maximum(total, 0.0).astype(BF)
    next_box = jnp.maximum(mm(first_box, v_bs[...]), 0.0).astype(BF)
    sc[...] = mm(next_box, w_bp[...])
    out_copy.wait()


def exchange(features):
    rows, cols = lax.axis_size("ty"), lax.axis_size("tx")

    def both(low_part, high_part, axis, count):
        forward = [(i, i + 1) for i in range(count - 1)]
        backward = [(j, i) for i, j in forward]
        return (lax.ppermute(high_part, axis, forward), lax.ppermute(low_part, axis, backward))

    top, bottom = both(features[:2], features[-2:], "ty", rows)
    low_cols = jnp.concatenate([top[:, :2], features[:, :2], bottom[:, :2]], axis=0)
    high_cols = jnp.concatenate([top[:, -2:], features[:, -2:], bottom[:, -2:]], axis=0)
    left, right = both(low_cols, high_cols, "tx", cols)
    left = jnp.pad(left, ((0, 1), (14, 0), (0, 0)))
    right = jnp.pad(right, ((1, 0), (0, 14), (0, 0)))
    return top, bottom, left + right


def on_device(
    features, block_reduce, block_spatial, block_expand, mask_first, mask_rest, mask_logit,
    box_reduce, box_hidden, box_second, box_predict, roi_anchor, roi_dest, roi_slot,
):
    anchor = roi_anchor[0, 0]
    base = anchor[:, :1] * TILE + anchor[:, 1:]
    logit_rows = jnp.broadcast_to(mask_logit[None, :], (8, MASK_CH))
    top, bottom, edge = exchange(features)
    hbm = pl.BlockSpec(memory_space=pl.ANY)
    vmem = pl.BlockSpec(memory_space=pltpu.VMEM)
    sec, lg, sc = pl.pallas_call(
        tile_kernel,
        out_shape=(
            jax.ShapeDtypeStruct((TILE, TILE, CH), BF),
            jax.ShapeDtypeStruct((CROP, 8, CROP * SLOTS), F32),
            jax.ShapeDtypeStruct((SLOTS, 5), F32),
        ),
        in_specs=[hbm] * 9 + [vmem] + [hbm] * 3 + [vmem, vmem],
        out_specs=(hbm, vmem, vmem),
        scratch_shapes=[
            pltpu.VMEM((TALL, WIDE, CH), BF),
            pltpu.VMEM((FLAT + 16, INNER), F32),
            pltpu.VMEM((TALL, WIDE, 3 * INNER), BF),
            pltpu.VMEM((3, TILE + 2, TILE, CH), BF),
            pltpu.VMEM((9, TILE + 2, TILE, MASK_CH), BF),
            pltpu.VMEM((9, 8 * TILE, MASK_CH), F32),
            pltpu.VMEM((TILE * TILE + 40, BOX_CH), F32),
            pltpu.VMEM((TILE, TILE, BOX_CH), BF),
            pltpu.VMEM((CROP, SLOTS, SPAN), BF),
            pltpu.VMEM((2, CROP - 2, SLOTS, TILE * TILE), BF),
            pltpu.VMEM((16, 16, SLOTS, MASK_CH), BF),
            pltpu.VMEM((16, 16, SLOTS, MASK_CH), BF),
            pltpu.VMEM((SLOTS, CROP // 2 * BOX_CH), BF),
            pltpu.VMEM((2, CH, INNER), BF),
            pltpu.VMEM((2, 9 * INNER, INNER), BF),
            pltpu.VMEM((2, INNER, CH), BF),
            pltpu.VMEM((9, CH, MASK_CH), BF),
            pltpu.VMEM((3, 9 * MASK_CH, MASK_CH), BF),
            pltpu.VMEM((CH, BOX_CH), BF),
            pltpu.VMEM(((CROP // 2) ** 2 * BOX_CH, FC), BF),
            pltpu.VMEM((FC, FC), BF),
            pltpu.SemaphoreType.DMA((13,)),
        ],
        compiler_params=pltpu.CompilerParams(vmem_limit_bytes=62 * 1024 * 1024),
        name="tile_heads",
    )(
        features, top, bottom, edge,
        block_reduce, block_spatial.reshape(2, 9 * INNER, INNER), block_expand,
        mask_first, mask_rest.reshape(3, 9 * MASK_CH, MASK_CH), logit_rows,
        box_reduce, box_hidden, box_second, box_predict, base,
    )
    used = (roi_dest[0, 0] >= 0)[:, None]
    logits = lg[:, 0].reshape(CROP * CROP, SLOTS).T
    logits = jnp.where(used, logits, 0.0)
    scores = jnp.where(used, sc, 0.0)
    return sec, logits[None, None], scores[None, None]


def solution(mesh):
    whole = P()
    in_specs = (P("ty", "tx", None),) + (whole,) * 10 + (
        P("ty", "tx", None, None), P("ty", "tx", None), P("ty", "tx", None),
    )
    out_specs = (P("ty", "tx", None), P("ty", "tx", None, None), P("ty", "tx", None, None))
    return jax.shard_map(
        on_device, mesh=mesh, in_specs=in_specs, out_specs=out_specs, check_vma=False
    )
```

```python
import jax
import jax.numpy as jnp
from jax import lax
from jax.experimental import pallas as pl
from jax.experimental.pallas import tpu as pltpu
from jax.sharding import PartitionSpec as P

CROP = 14
TILE = 32
WIDE = 48
TALL = 37
FLAT = TALL * WIDE
CH = 512
INNER = 128
MASK_CH = 256
BOX_CH = 128
FC = 1024
SLOTS = 32
WINDOW = 20
SPAN = WINDOW * TILE
BF = jnp.bfloat16
F32 = jnp.float32


def mm(a, b):
    return jnp.dot(a, b, preferred_element_type=F32)


def tile_kernel(
    feat, top, bottom, edge, w_red, w_spa, w_exp, w_first, w_rest, w_log, w_br, w_bh, w_bs, w_bp,
    base, used,
    sec, lg, sc,
    xe, inr, cat, xs, mv, taps, redf, avg, pick, pick_side, ma, mb, prod, box_t,
    v_red, v_spa, v_exp, v_first, v_rest, v_br, v_bh, v_bs,
    sems,
):
    row_at = lax.axis_index("ty")
    col_at = lax.axis_index("tx")
    rows_of = lax.axis_size("ty")
    cols_of = lax.axis_size("tx")

    copies = [
        pltpu.make_async_copy(feat, xe.at[3:35, 0:TILE], sems.at[0]),
        pltpu.make_async_copy(top, xe.at[1:3, 0:TILE], sems.at[1]),
        pltpu.make_async_copy(bottom, xe.at[35:37, 0:TILE], sems.at[2]),
        pltpu.make_async_copy(edge, xe.at[0:TALL, TILE:WIDE], sems.at[3]),
        pltpu.make_async_copy(w_red, v_red, sems.at[4]),
        pltpu.make_async_copy(w_spa, v_spa, sems.at[5]),
        pltpu.make_async_copy(w_exp, v_exp, sems.at[6]),
        pltpu.make_async_copy(w_first, v_first, sems.at[7]),
        pltpu.make_async_copy(w_br, v_br, sems.at[8]),
        pltpu.make_async_copy(w_rest, v_rest, sems.at[9]),
        pltpu.make_async_copy(w_bh, v_bh, sems.at[10]),
        pltpu.make_async_copy(w_bs, v_bs, sems.at[11]),
    ]
    for copy in copies:
        copy.start()

    xe[0:1, 0:TILE, :] = jnp.zeros((1, TILE, CH), BF)
    inr[0:8, :] = jnp.zeros((8, INNER), F32)
    inr[8 + FLAT : 16 + FLAT, :] = jnp.zeros((8, INNER), F32)
    for j in range(3):
        xs[j, 0, :, :] = jnp.zeros((TILE, CH), BF)
        xs[j, TILE + 1, :, :] = jnp.zeros((TILE, CH), BF)
    for v in range(9):
        mv[v, TILE : TILE + 2, :, :] = jnp.zeros((2, TILE, MASK_CH), BF)
    redf[TILE * TILE : TILE * TILE + 40, :] = jnp.zeros((40, BOX_CH), F32)
    line = jnp.zeros((8, SLOTS, MASK_CH), BF)
    for ref in (ma, mb):
        for parity in range(2):
            ref[0, parity] = line
            ref[15, parity] = line
        for r in range(1, 15):
            ref[r, 0, 0] = line[0]
            ref[r, 1, 7] = line[0]

    at = base[...]
    lanes = lax.broadcasted_iota(jnp.int32, (SLOTS, SPAN), 1) - at
    for k, c in enumerate([*range(0, CROP, 2), *range(1, CROP, 2)]):
        pick[k] = jnp.where(lanes == c, 1.0, 0.0).astype(BF)
    lanes = lax.broadcasted_iota(jnp.int32, (SLOTS, TILE * TILE), 1) - at
    for side, c in enumerate((0, CROP - 1)):
        for r in range(1, CROP - 1):
            pick_side[side, r - 1] = jnp.where(lanes == r * TILE + c, 1.0, 0.0).astype(BF)

    for copy in copies[:7]:
        copy.wait()

    for b in range(2):
        def reduce_rows(k, _):
            x = xe[pl.ds(k * 4, 4)].reshape(4 * WIDE, CH)
            h = jnp.maximum(mm(x, v_red[b]), 0.0)
            inr[pl.ds(pl.multiple_of(8 + k * 4 * WIDE, 8), 4 * WIDE), :] = h
            return 0

        lax.fori_loop(0, 9, reduce_rows, 0, unroll=True)
        x = xe[36:37].reshape(WIDE, CH)
        inr[8 + 36 * WIDE : 8 + FLAT, :] = jnp.maximum(mm(x, v_red[b]), 0.0)

        if b == 1:
            @pl.when(row_at == 0)
            def _():
                inr[8 + 2 * WIDE - 2 : 8 + 3 * WIDE - 2, :] = jnp.zeros((WIDE, INNER), F32)

            @pl.when(row_at == rows_of - 1)
            def _():
                inr[8 + 35 * WIDE - 2 : 8 + 36 * WIDE - 2, :] = jnp.zeros((WIDE, INNER), F32)

            @pl.when(col_at == 0)
            def _():
                inr[pl.ds(8 + WIDE - 1, TALL, stride=WIDE), :] = jnp.zeros((TALL, INNER), F32)

            @pl.when(col_at == cols_of - 1)
            def _():
                inr[pl.ds(8 + TILE, TALL, stride=WIDE), :] = jnp.zeros((TALL, INNER), F32)

        def shift_rows(k, _):
            here = pl.multiple_of(k * WIDE, 8)
            block = inr[pl.ds(here, WIDE + 16), :]
            for j in range(3):
                cat[k, :, j * INNER : (j + 1) * INNER] = block[7 + j : 7 + j + WIDE].astype(BF)
            return 0

        lax.fori_loop(0, TALL, shift_rows, 0, unroll=True)

        count = 5 if b == 0 else 4
        per = 7 if b == 0 else 8
        first = 1 if b == 0 else 3

        def spatial_rows(k, _):
            r = first + k * per
            lhs = jnp.concatenate([cat[pl.ds(r + i - 1, per)] for i in range(3)], axis=2)
            s = jnp.maximum(mm(lhs.reshape(per * WIDE, 9 * INNER), v_spa[b]), 0.0).astype(BF)
            y = mm(s, v_exp[b]) + xe[pl.ds(r, per)].reshape(per * WIDE, CH).astype(F32)
            y = jnp.maximum(y, 0.0).astype(BF)
            if b == 0:
                xe[pl.ds(r, per)] = y.reshape(per, WIDE, CH)
            else:
                xs[1, pl.ds(r - 2, per)] = y.reshape(per, WIDE, CH)[:, :TILE]
                wide = y.astype(F32)
                low = pltpu.roll(wide, 1, 0).reshape(per, WIDE, CH)[:, :TILE]
                high = pltpu.roll(wide, per * WIDE - 1, 0).reshape(per, WIDE, CH)[:, :TILE]
                xs[0, pl.ds(r - 2, per)] = low.astype(BF)
                xs[2, pl.ds(r - 2, per)] = high.astype(BF)
            return 0

        lax.fori_loop(0, count, spatial_rows, 0, unroll=True)

    out_copy = pltpu.make_async_copy(xs.at[1, 1 : TILE + 1], sec, sems.at[12])
    out_copy.start()
    copies[7].wait()
    copies[8].wait()

    def stem_rows(k, _):
        r = k * 8
        for i in range(3):
            for j in range(3):
                lhs = xs[j, pl.ds(r + i, 8)].reshape(8 * TILE, CH)
                taps[3 * i + j] = mm(lhs, v_first[3 * i + j])
        sums = []
        for i in range(3):
            t0, t1, t2 = taps[3 * i], taps[3 * i + 1], taps[3 * i + 2]
            right = t0 + t1
            sums.append((t1 + t2, right + t2, right))
        for cv in range(3):
            a0, a1, a2 = sums[0][cv], sums[1][cv], sums[2][cv]
            low = a0 + a1
            for rv, value in enumerate((a1 + a2, low + a2, low)):
                value = jnp.maximum(value, 0.0).astype(BF).reshape(8, TILE, MASK_CH)
                mv[3 * rv + cv, pl.ds(r, 8)] = value
        red = mm(xs[1, pl.ds(r + 1, 8)].reshape(8 * TILE, CH), v_br[...])
        redf[pl.ds(pl.multiple_of(r * TILE, 8), 8 * TILE), :] = red
        return 0

    lax.fori_loop(0, 4, stem_rows, 0, unroll=True)

    def average_rows(k, _):
        here = pl.multiple_of(k * 4 * TILE, 8)
        block = redf[pl.ds(here, 5 * TILE + 8), :]
        pair = block[: 5 * TILE] + block[1 : 5 * TILE + 1]
        quad = (pair[: 4 * TILE] + pair[TILE:]) * 0.25
        avg[pl.ds(k * 4, 4)] = quad.astype(BF).reshape(4, TILE, BOX_CH)
        return 0

    lax.fori_loop(0, 8, average_rows, 0, unroll=True)

    inside = CROP - 2

    def choose(picker, source):
        return mm(picker, source).astype(BF)

    def table(v, r):
        return mv[v, pl.ds(r, WINDOW)].reshape(SPAN, MASK_CH)

    last = CROP - 1
    half = CROP // 2

    def gather_inside(r, v):
        got = choose(pick[1:last].reshape(inside * SLOTS, SPAN), table(v, r))
        got = got.reshape(2, half - 1, SLOTS, MASK_CH)
        ma[r + 1, 1, 1:half] = got[0]
        ma[r + 1, 0, 1:half] = got[1]

    def gather_row(r, _):
        gather_inside(r, 4)
        return 0

    lax.fori_loop(1, last, gather_row, 0, unroll=True)
    for r, v in ((0, 1), (last, 7)):
        gather_inside(r, v)
        ma[r + 1, 1, 0] = choose(pick[0], table(v - 1, r))
        ma[r + 1, 0, half] = choose(pick[last], table(v + 1, r))
    for side, v in ((0, 3), (1, 5)):
        got = choose(
            pick_side[side].reshape(inside * SLOTS, TILE * TILE),
            mv[v, 0:TILE].reshape(TILE * TILE, MASK_CH),
        )
        ma[2:CROP, 1 - side, side * half] = got.reshape(inside, SLOTS, MASK_CH)

    copies[9].wait()

    def parity_rows(layer, source, target, t):
        d0, d1, d2, d3 = (source[2 * t + k] for k in range(4))
        for xi, w in enumerate((d0 - d2, d1 + d2, d2 - d1, d1 - d3)):
            even, odd = w[0], w[1]
            e0, e1, o0, o1 = even[:half], even[1:], odd[:half], odd[1:]
            for nu, v in enumerate((e0 - e1, o0 + e1, e1 - o0, o0 - o1)):
                k = 4 * xi + nu
                prod[k] = mm(v.reshape(half * SLOTS, MASK_CH), v_rest[layer, k])
        lines = []
        for xi in range(4):
            m0, m1, m2, m3 = (prod[4 * xi + nu] for nu in range(4))
            lines.append((m0 + m1 + m2, m1 - m2 - m3))
        for b in range(2):
            y0, y1, y2, y3 = (lines[xi][b] for xi in range(4))
            for a, y in enumerate((y0 + y1 + y2, y1 - y2 - y3)):
                y = jnp.maximum(y, 0.0).astype(BF).reshape(half, SLOTS, MASK_CH)
                target[2 * t + a + 1, 1 - b, b : b + half] = y

    for layer in range(3):
        source, target = (ma, mb) if layer % 2 == 0 else (mb, ma)

        def conv_rows(t, _):
            parity_rows(layer, source, target, t)
            return 0

        lax.fori_loop(0, half, conv_rows, 0, unroll=True)

    cell_lane = lax.broadcasted_iota(jnp.int32, (SLOTS, 256), 1)

    def logit_rows(r, total):
        for parity in range(2):
            act = mb[r + 1, parity, 1 - parity : 1 - parity + half]
            got = mm(act.reshape(half * SLOTS, MASK_CH), w_log[...])
            for u in range(half):
                part = got[u * SLOTS : (u + 1) * SLOTS]
                cell = r * CROP + 2 * u + 1 - parity
                total = jnp.where(cell_lane == cell, jnp.concatenate([part, part], axis=1), total)
        return total

    total = lax.fori_loop(0, CROP, logit_rows, jnp.zeros((SLOTS, 256), F32), unroll=True)
    total = jnp.where(used[...] > 0, total, 0.0)
    lg[0, 0] = total[:, : CROP * CROP]

    copies[10].wait()
    copies[11].wait()
    even = pick[0:half].reshape(half * SLOTS, SPAN)

    def box_row(t, total):
        got = choose(even, avg[pl.ds(2 * t, WINDOW)].reshape(SPAN, BOX_CH))
        for u in range(half):
            box_t[:, u * BOX_CH : (u + 1) * BOX_CH] = got[u * SLOTS : (u + 1) * SLOTS]
        part = v_bh[pl.ds(pl.multiple_of(t * half * BOX_CH, BOX_CH), half * BOX_CH), :]
        return total + mm(box_t[...], part)

    total = lax.fori_loop(0, half, box_row, jnp.zeros((SLOTS, FC), F32), unroll=True)
    first_box = jnp.maximum(total, 0.0).astype(BF)
    next_box = jnp.maximum(mm(first_box, v_bs[...]), 0.0).astype(BF)
    scores = lax.dot_general(
        next_box, w_bp[...], (((1,), (1,)), ((), ())), preferred_element_type=F32
    )
    sc[0, 0] = jnp.where(used[...] > 0, scores, 0.0)
    out_copy.wait()


def weights_kernel(w, u):
    def spread(a, b, c):
        even, odd = (a + c) * 0.5, b * 0.5
        return a, even + odd, even - odd, c

    taps = [w[0, k].astype(F32) for k in range(9)]
    rows = [spread(taps[j], taps[3 + j], taps[6 + j]) for j in range(3)]
    for xi in range(4):
        for nu, value in enumerate(spread(rows[0][xi], rows[1][xi], rows[2][xi])):
            u[0, 4 * xi + nu] = value.astype(BF)


def transform_weights(mask_rest):
    step = 64
    return pl.pallas_call(
        weights_kernel,
        grid=(3, MASK_CH // step),
        out_shape=jax.ShapeDtypeStruct((3, 16, MASK_CH, MASK_CH), BF),
        in_specs=[pl.BlockSpec((1, 9, step, MASK_CH), lambda l, k: (l, 0, k, 0))],
        out_specs=pl.BlockSpec((1, 16, step, MASK_CH), lambda l, k: (l, 0, k, 0)),
        cost_estimate=pl.CostEstimate(
            flops=3 * 16 * 3 * MASK_CH * MASK_CH,
            bytes_accessed=3 * 25 * 2 * MASK_CH * MASK_CH,
            transcendentals=0,
        ),
        name="filter_weights",
    )(mask_rest)


def exchange(features):
    rows, cols = lax.axis_size("ty"), lax.axis_size("tx")

    def both(low_part, high_part, axis, count):
        forward = [(i, i + 1) for i in range(count - 1)]
        backward = [(j, i) for i, j in forward]
        return (lax.ppermute(high_part, axis, forward), lax.ppermute(low_part, axis, backward))

    top, bottom = both(features[:2], features[-2:], "ty", rows)
    low_cols = jnp.concatenate([top[:, :2], features[:, :2], bottom[:, :2]], axis=0)
    high_cols = jnp.concatenate([top[:, -2:], features[:, -2:], bottom[:, -2:]], axis=0)
    left, right = both(low_cols, high_cols, "tx", cols)
    left = jnp.pad(left, ((0, 1), (14, 0), (0, 0)))
    right = jnp.pad(right, ((1, 0), (0, 14), (0, 0)))
    return top, bottom, left + right


def on_device(
    features, block_reduce, block_spatial, block_expand, mask_first, mask_rest, mask_logit,
    box_reduce, box_hidden, box_second, box_predict, roi_anchor, roi_dest, roi_slot,
):
    anchor = roi_anchor[0, 0]
    base = anchor[:, :1] * TILE + anchor[:, 1:]
    logit_column = jnp.broadcast_to(mask_logit[:, None], (MASK_CH, 128))
    used = (roi_dest[0, 0] >= 0)[:, None].astype(jnp.int32)
    top, bottom, edge = exchange(features)
    hbm = pl.BlockSpec(memory_space=pl.ANY)
    vmem = pl.BlockSpec(memory_space=pltpu.VMEM)
    sec, lg, sc = pl.pallas_call(
        tile_kernel,
        out_shape=(
            jax.ShapeDtypeStruct((TILE, TILE, CH), BF),
            jax.ShapeDtypeStruct((1, 1, SLOTS, CROP * CROP), F32),
            jax.ShapeDtypeStruct((1, 1, SLOTS, 5), F32),
        ),
        in_specs=[hbm] * 9 + [vmem] + [hbm] * 3 + [vmem, vmem, vmem],
        out_specs=(hbm, vmem, vmem),
        scratch_shapes=[
            pltpu.VMEM((TALL, WIDE, CH), BF),
            pltpu.VMEM((FLAT + 16, INNER), F32),
            pltpu.VMEM((TALL, WIDE, 3 * INNER), BF),
            pltpu.VMEM((3, TILE + 2, TILE, CH), BF),
            pltpu.VMEM((9, TILE + 2, TILE, MASK_CH), BF),
            pltpu.VMEM((9, 8 * TILE, MASK_CH), F32),
            pltpu.VMEM((TILE * TILE + 40, BOX_CH), F32),
            pltpu.VMEM((TILE, TILE, BOX_CH), BF),
            pltpu.VMEM((CROP, SLOTS, SPAN), BF),
            pltpu.VMEM((2, CROP - 2, SLOTS, TILE * TILE), BF),
            pltpu.VMEM((16, 2, 8, SLOTS, MASK_CH), BF),
            pltpu.VMEM((16, 2, 8, SLOTS, MASK_CH), BF),
            pltpu.VMEM((16, 7 * SLOTS, MASK_CH), F32),
            pltpu.VMEM((SLOTS, CROP // 2 * BOX_CH), BF),
            pltpu.VMEM((2, CH, INNER), BF),
            pltpu.VMEM((2, 9 * INNER, INNER), BF),
            pltpu.VMEM((2, INNER, CH), BF),
            pltpu.VMEM((9, CH, MASK_CH), BF),
            pltpu.VMEM((3, 16, MASK_CH, MASK_CH), BF),
            pltpu.VMEM((CH, BOX_CH), BF),
            pltpu.VMEM(((CROP // 2) ** 2 * BOX_CH, FC), BF),
            pltpu.VMEM((FC, FC), BF),
            pltpu.SemaphoreType.DMA((13,)),
        ],
        compiler_params=pltpu.CompilerParams(vmem_limit_bytes=62 * 1024 * 1024),
        name="tile_heads",
    )(
        features, top, bottom, edge,
        block_reduce, block_spatial.reshape(2, 9 * INNER, INNER), block_expand,
        mask_first, transform_weights(mask_rest), logit_column,
        box_reduce, box_hidden, box_second, box_predict.T, base, used,
    )
    return sec, lg, sc


def solution(mesh):
    whole = P()
    in_specs = (P("ty", "tx", None),) + (whole,) * 10 + (
        P("ty", "tx", None, None), P("ty", "tx", None), P("ty", "tx", None),
    )
    out_specs = (P("ty", "tx", None), P("ty", "tx", None, None), P("ty", "tx", None, None))
    return jax.shard_map(
        on_device, mesh=mesh, in_specs=in_specs, out_specs=out_specs, check_vma=False
    )
```

```python
import jax
import jax.numpy as jnp
from jax import lax
from jax.experimental import pallas as pl
from jax.experimental.pallas import tpu as pltpu
from jax.sharding import PartitionSpec as P

CROP = 14
TILE = 32
WIDE = 48
TALL = 36
CH = 512
INNER = 128
MASK_CH = 256
BOX_CH = 128
FC = 1024
SLOTS = 32
WINDOW = 20
SPAN = WINDOW * TILE
BF = jnp.bfloat16
F32 = jnp.float32


def mm(a, b):
    return jnp.dot(a, b, preferred_element_type=F32)


def tile_kernel(
    feat, top, bottom, edge, w_red, w_spa, w_exp, w_first, w_rest, w_log, w_br, w_bh, w_bs, w_bp,
    anchor, dest,
    sec, lg, sc,
    xe, inr, cat, xs, mv, taps, redf, avg, pick, pick_side, ma, mb, prod, box_t,
    v_red, v_spa, v_exp, v_first, v_rest, v_br, v_bh, v_bs,
    sems,
):
    row_at = lax.axis_index("ty")
    col_at = lax.axis_index("tx")
    rows_of = lax.axis_size("ty")
    cols_of = lax.axis_size("tx")

    copies = [
        pltpu.make_async_copy(feat, xe.at[2:34, 0:TILE], sems.at[0]),
        pltpu.make_async_copy(top, xe.at[0:2], sems.at[1]),
        pltpu.make_async_copy(bottom, xe.at[34:36], sems.at[2]),
        pltpu.make_async_copy(edge, xe.at[2:34, TILE:WIDE], sems.at[3]),
        pltpu.make_async_copy(w_red, v_red, sems.at[4]),
        pltpu.make_async_copy(w_spa, v_spa, sems.at[5]),
        pltpu.make_async_copy(w_exp, v_exp, sems.at[6]),
        pltpu.make_async_copy(w_first, v_first, sems.at[7]),
        pltpu.make_async_copy(w_br, v_br, sems.at[8]),
        pltpu.make_async_copy(w_rest, v_rest, sems.at[9]),
        pltpu.make_async_copy(w_bh, v_bh, sems.at[10]),
        pltpu.make_async_copy(w_bs, v_bs, sems.at[11]),
    ]
    for copy in copies:
        copy.start()

    for j in range(3):
        xs[j, 0, :, :] = jnp.zeros((TILE, CH), BF)
        xs[j, TILE + 1, :, :] = jnp.zeros((TILE, CH), BF)
    for v in range(9):
        mv[v, TILE : TILE + 2, :, :] = jnp.zeros((2, TILE, MASK_CH), BF)
    redf[TILE * TILE : TILE * TILE + 40, :] = jnp.zeros((40, BOX_CH), F32)
    line = jnp.zeros((8, SLOTS, MASK_CH), BF)
    for ref in (ma, mb):
        for parity in range(2):
            ref[0, parity] = line
            ref[15, parity] = line
        for r in range(1, 15):
            ref[r, 0, 0] = line[0]
            ref[r, 1, 7] = line[0]

    def column(row):
        return jnp.broadcast_to(row.astype(F32), (SLOTS, SLOTS)).T[:, :1].astype(jnp.int32)

    used = dest[...] >= 0
    used_column = column(used)
    at = column(anchor[0:1] * TILE + anchor[1:2])
    log_w = jnp.broadcast_to(w_log[...].astype(F32), (128, MASK_CH)).T.astype(BF)
    lanes = lax.broadcasted_iota(jnp.int32, (SLOTS, SPAN), 1) - at
    for k, c in enumerate([*range(0, CROP, 2), *range(1, CROP, 2)]):
        pick[k] = jnp.where(lanes == c, 1.0, 0.0).astype(BF)
    lanes = lax.broadcasted_iota(jnp.int32, (SLOTS, TILE * TILE), 1) - at
    for side, c in enumerate((0, CROP - 1)):
        for r in range(1, CROP - 1):
            pick_side[side, r - 1] = jnp.where(lanes == r * TILE + c, 1.0, 0.0).astype(BF)

    for copy in copies[:7]:
        copy.wait()

    first_row, last_row = row_at == 0, row_at == rows_of - 1
    first_col, last_col = col_at == 0, col_at == cols_of - 1

    for b in range(2):
        for r in range(0, TALL, 4):
            x = xe[r : r + 4].reshape(4 * WIDE, CH)
            inr[r : r + 4] = jnp.maximum(mm(x, v_red[b]), 0.0).reshape(4, WIDE, INNER)
        inr[0:2] = jnp.where(first_row, 0.0, inr[0:2])
        inr[34:36] = jnp.where(last_row, 0.0, inr[34:36])
        inr[:, 40:48] = jnp.where(first_col, 0.0, inr[:, 40:48])
        inr[:, 32:40] = jnp.where(last_col, 0.0, inr[:, 32:40])

        for r in range(TALL):
            line = inr[r]
            cat[r, :, :INNER] = pltpu.roll(line, 1, 0).astype(BF)
            cat[r, :, INNER : 2 * INNER] = line.astype(BF)
            cat[r, :, 2 * INNER :] = pltpu.roll(line, WIDE - 1, 0).astype(BF)

        for r, per in ((1, 7), (8, 7), (15, 7), (22, 7), (29, 6)) if b == 0 else (
            (2, 8), (10, 8), (18, 8), (26, 8)
        ):
            lhs = jnp.concatenate([cat[r + i - 1 : r + i - 1 + per] for i in range(3)], axis=2)
            h = jnp.maximum(mm(lhs.reshape(per * WIDE, 9 * INNER), v_spa[b]), 0.0).astype(BF)
            y = mm(h, v_exp[b]) + xe[r : r + per].reshape(per * WIDE, CH).astype(F32)
            y = jnp.maximum(y, 0.0).astype(BF).reshape(per, WIDE, CH)
            if b == 0:
                xe[r : r + per] = y
            else:
                y = y[:, :TILE]
                xs[1, r - 1 : r - 1 + per] = y
                flat = y.reshape(per * TILE, CH).astype(F32)
                for j, shift in ((0, 1), (2, per * TILE - 1)):
                    moved = pltpu.roll(flat, shift, 0).astype(BF)
                    xs[j, r - 1 : r - 1 + per] = moved.reshape(per, TILE, CH)

    out_copy = pltpu.make_async_copy(xs.at[1, 1 : TILE + 1], sec, sems.at[12])
    out_copy.start()
    copies[7].wait()
    copies[8].wait()

    def stem_rows(k, _):
        r = k * 8
        for i in range(3):
            for j in range(3):
                lhs = xs[j, pl.ds(r + i, 8)].reshape(8 * TILE, CH)
                taps[3 * i + j] = mm(lhs, v_first[3 * i + j])
        sums = []
        for i in range(3):
            t0, t1, t2 = taps[3 * i], taps[3 * i + 1], taps[3 * i + 2]
            right = t0 + t1
            sums.append((t1 + t2, right + t2, right))
        for cv in range(3):
            a0, a1, a2 = sums[0][cv], sums[1][cv], sums[2][cv]
            low = a0 + a1
            for rv, value in enumerate((a1 + a2, low + a2, low)):
                value = jnp.maximum(value, 0.0).astype(BF).reshape(8, TILE, MASK_CH)
                mv[3 * rv + cv, pl.ds(r, 8)] = value
        red = mm(xs[1, pl.ds(r + 1, 8)].reshape(8 * TILE, CH), v_br[...])
        redf[pl.ds(pl.multiple_of(r * TILE, 8), 8 * TILE), :] = red
        return 0

    for k in range(4):
        stem_rows(k, 0)

    def average_rows(k, _):
        here = pl.multiple_of(k * 4 * TILE, 8)
        block = redf[pl.ds(here, 5 * TILE + 8), :]
        pair = block[: 5 * TILE] + block[1 : 5 * TILE + 1]
        quad = (pair[: 4 * TILE] + pair[TILE:]) * 0.25
        avg[pl.ds(k * 4, 4)] = quad.astype(BF).reshape(4, TILE, BOX_CH)
        return 0

    lax.fori_loop(0, 8, average_rows, 0, unroll=True)

    inside = CROP - 2

    def choose(picker, source):
        return mm(picker, source).astype(BF)

    def table(v, r):
        return mv[v, pl.ds(r, WINDOW)].reshape(SPAN, MASK_CH)

    last = CROP - 1
    half = CROP // 2

    def gather_inside(r, v):
        got = choose(pick[1:last].reshape(inside * SLOTS, SPAN), table(v, r))
        got = got.reshape(2, half - 1, SLOTS, MASK_CH)
        ma[r + 1, 1, 1:half] = got[0]
        ma[r + 1, 0, 1:half] = got[1]

    def gather_row(r, _):
        gather_inside(r, 4)
        return 0

    lax.fori_loop(1, last, gather_row, 0, unroll=True)
    for r, v in ((0, 1), (last, 7)):
        gather_inside(r, v)
        ma[r + 1, 1, 0] = choose(pick[0], table(v - 1, r))
        ma[r + 1, 0, half] = choose(pick[last], table(v + 1, r))
    for side, v in ((0, 3), (1, 5)):
        got = choose(
            pick_side[side].reshape(inside * SLOTS, TILE * TILE),
            mv[v, 0:TILE].reshape(TILE * TILE, MASK_CH),
        )
        ma[2:CROP, 1 - side, side * half] = got.reshape(inside, SLOTS, MASK_CH)

    for copy in copies[9:12]:
        copy.wait()

    def filtered(layer, source, t):
        d0, d1, d2, d3 = (source[2 * t + k] for k in range(4))
        for xi, w in enumerate((d0 - d2, d1 + d2, d2 - d1, d1 - d3)):
            even, odd = w[0], w[1]
            e0, e1, o0, o1 = even[:half], even[1:], odd[:half], odd[1:]
            for nu, v in enumerate((e0 - e1, o0 + e1, e1 - o0, o0 - o1)):
                k = 4 * xi + nu
                prod[k] = mm(v.reshape(half * SLOTS, MASK_CH), v_rest[layer, k])
        lines = []
        for xi in range(4):
            m0, m1, m2, m3 = (prod[4 * xi + nu] for nu in range(4))
            lines.append((m0 + m1 + m2, m1 - m2 - m3))
        for b in range(2):
            y0, y1, y2, y3 = (lines[xi][b] for xi in range(4))
            for a, y in enumerate((y0 + y1 + y2, y1 - y2 - y3)):
                yield a, b, jnp.maximum(y, 0.0).astype(BF)

    cell_lane = lax.broadcasted_iota(jnp.int32, (SLOTS, 256), 1)
    logits = jnp.zeros((SLOTS, 256), F32)
    total = jnp.zeros((SLOTS, FC), F32)
    even = pick[0:half].reshape(half * SLOTS, SPAN)

    for layer in range(3):
        source, target = (ma, mb) if layer % 2 == 0 else (mb, ma)
        for t in range(half):
            for a, b, act in filtered(layer, source, t):
                if layer < 2:
                    act = act.reshape(half, SLOTS, MASK_CH)
                    target[2 * t + a + 1, 1 - b, b : b + half] = act
                    continue
                got = mm(act, log_w)
                for u in range(half):
                    part = got[u * SLOTS : (u + 1) * SLOTS]
                    cell = (2 * t + a) * CROP + 2 * u + b
                    wide = jnp.concatenate([part, part], axis=1)
                    logits = jnp.where(cell_lane == cell, wide, logits)
            if layer == 0:
                got = choose(even, avg[2 * t : 2 * t + WINDOW].reshape(SPAN, BOX_CH))
                for u in range(half):
                    box_t[t, :, u * BOX_CH : (u + 1) * BOX_CH] = got[u * SLOTS : (u + 1) * SLOTS]
            if layer == 1:
                part = v_bh[t * half * BOX_CH : (t + 1) * half * BOX_CH, :]
                total = total + mm(box_t[t], part)
    logits = jnp.where(used_column > 0, logits, 0.0)
    lg[0, 0] = logits[:, : CROP * CROP]

    first_box = jnp.maximum(total, 0.0).astype(BF)
    next_box = jnp.maximum(mm(first_box, v_bs[...]), 0.0).astype(BF)
    scores = lax.dot_general(
        w_bp[...], next_box, (((1,), (1,)), ((), ())), preferred_element_type=F32
    )
    scores = jnp.where(used, scores, 0.0)
    for k in range(5):
        sc[0, k] = scores[k : k + 1]
    out_copy.wait()


def weights_kernel(w, u):
    def spread(a, b, c):
        even, odd = (a + c) * 0.5, b * 0.5
        return a, even + odd, even - odd, c

    taps = [w[0, k].astype(F32) for k in range(9)]
    rows = [spread(taps[j], taps[3 + j], taps[6 + j]) for j in range(3)]
    for xi in range(4):
        for nu, value in enumerate(spread(rows[0][xi], rows[1][xi], rows[2][xi])):
            u[0, 4 * xi + nu] = value.astype(BF)


def transform_weights(mask_rest):
    step = 128
    return pl.pallas_call(
        weights_kernel,
        grid=(3, MASK_CH // step),
        out_shape=jax.ShapeDtypeStruct((3, 16, MASK_CH, MASK_CH), BF),
        in_specs=[pl.BlockSpec((1, 9, step, MASK_CH), lambda l, k: (l, 0, k, 0))],
        out_specs=pl.BlockSpec((1, 16, step, MASK_CH), lambda l, k: (l, 0, k, 0)),
        cost_estimate=pl.CostEstimate(
            flops=3 * 16 * 3 * MASK_CH * MASK_CH,
            bytes_accessed=3 * 25 * 2 * MASK_CH * MASK_CH,
            transcendentals=0,
        ),
        name="filter_weights",
    )(mask_rest)


def exchange(features):
    rows, cols = lax.axis_size("ty"), lax.axis_size("tx")

    def send(part, down, right):
        pairs = [
            (r * cols + c, (r + down) % rows * cols + (c + right) % cols)
            for r in range(rows)
            for c in range(cols)
        ]
        return lax.ppermute(part, ("ty", "tx"), pairs)

    left = send(features[:, -2:], 0, 1)
    right = send(features[:, :2], 0, -1)
    edge = jnp.pad(left, ((0, 0), (14, 0), (0, 0))) + jnp.pad(right, ((0, 0), (0, 14), (0, 0)))
    top = send(jnp.concatenate([features[-2:], edge[-2:]], axis=1), 1, 0)
    bottom = send(jnp.concatenate([features[:2], edge[:2]], axis=1), -1, 0)
    return top, bottom, edge


def on_device(
    features, block_reduce, block_spatial, block_expand, mask_first, mask_rest, mask_logit,
    box_reduce, box_hidden, box_second, box_predict, roi_anchor, roi_dest, roi_slot,
):
    top, bottom, edge = exchange(features)
    hbm = pl.BlockSpec(memory_space=pl.ANY)
    vmem = pl.BlockSpec(memory_space=pltpu.VMEM)
    sec, lg, sc = pl.pallas_call(
        tile_kernel,
        out_shape=(
            jax.ShapeDtypeStruct((TILE, TILE, CH), BF),
            jax.ShapeDtypeStruct((1, 1, SLOTS, CROP * CROP), F32),
            jax.ShapeDtypeStruct((1, 5, 1, SLOTS), F32),
        ),
        in_specs=[hbm] * 9 + [vmem] + [hbm] * 3 + [vmem, vmem, vmem],
        out_specs=(hbm, vmem, vmem),
        scratch_shapes=[
            pltpu.VMEM((TALL, WIDE, CH), BF),
            pltpu.VMEM((TALL, WIDE, INNER), F32),
            pltpu.VMEM((TALL, WIDE, 3 * INNER), BF),
            pltpu.VMEM((3, TILE + 2, TILE, CH), BF),
            pltpu.VMEM((9, TILE + 2, TILE, MASK_CH), BF),
            pltpu.VMEM((9, 8 * TILE, MASK_CH), F32),
            pltpu.VMEM((TILE * TILE + 40, BOX_CH), F32),
            pltpu.VMEM((TILE, TILE, BOX_CH), BF),
            pltpu.VMEM((CROP, SLOTS, SPAN), BF),
            pltpu.VMEM((2, CROP - 2, SLOTS, TILE * TILE), BF),
            pltpu.VMEM((16, 2, 8, SLOTS, MASK_CH), BF),
            pltpu.VMEM((16, 2, 8, SLOTS, MASK_CH), BF),
            pltpu.VMEM((16, 7 * SLOTS, MASK_CH), F32),
            pltpu.VMEM((CROP // 2, SLOTS, CROP // 2 * BOX_CH), BF),
            pltpu.VMEM((2, CH, INNER), BF),
            pltpu.VMEM((2, 9 * INNER, INNER), BF),
            pltpu.VMEM((2, INNER, CH), BF),
            pltpu.VMEM((9, CH, MASK_CH), BF),
            pltpu.VMEM((3, 16, MASK_CH, MASK_CH), BF),
            pltpu.VMEM((CH, BOX_CH), BF),
            pltpu.VMEM(((CROP // 2) ** 2 * BOX_CH, FC), BF),
            pltpu.VMEM((FC, FC), BF),
            pltpu.SemaphoreType.DMA((13,)),
        ],
        compiler_params=pltpu.CompilerParams(vmem_limit_bytes=62 * 1024 * 1024),
        name="tile_heads",
    )(
        features, top, bottom, edge,
        block_reduce, block_spatial.reshape(2, 9 * INNER, INNER), block_expand,
        mask_first, transform_weights(mask_rest), mask_logit[None, :],
        box_reduce, box_hidden, box_second, box_predict.T, roi_anchor[0, 0].T, roi_dest[0],
    )
    return sec, lg, sc.transpose(0, 2, 3, 1)


def solution(mesh):
    whole = P()
    in_specs = (P("ty", "tx", None),) + (whole,) * 10 + (
        P("ty", "tx", None, None), P("ty", "tx", None), P("ty", "tx", None),
    )
    out_specs = (P("ty", "tx", None), P("ty", "tx", None, None), P("ty", "tx", None, None))
    return jax.shard_map(
        on_device, mesh=mesh, in_specs=in_specs, out_specs=out_specs, check_vma=False
    )
```

```python
import jax
import jax.numpy as jnp
from jax import lax
from jax.experimental import pallas as pl
from jax.experimental.pallas import tpu as pltpu
from jax.sharding import PartitionSpec as P

CROP = 14
TILE = 32
WIDE = 48
TALL = 36
CH = 512
INNER = 128
MASK_CH = 256
BOX_CH = 128
FC = 1024
SLOTS = 32
WINDOW = 20
GROUPS = ((0, 1), (2, 3), (4, 5), (6,))
SPAN = WINDOW * TILE
BF = jnp.bfloat16
F32 = jnp.float32


def mm(a, b):
    return jnp.dot(a, b, preferred_element_type=F32)


def spread(a, b, c):
    even, odd = (a + c) * 0.5, b * 0.5
    return a, even + odd, even - odd, c


def filter_weights(w, u, layer, part):
    taps = [w[layer, k, part].astype(F32) for k in range(9)]
    rows = [spread(taps[j], taps[3 + j], taps[6 + j]) for j in range(3)]
    for xi in range(4):
        for nu, value in enumerate(spread(rows[0][xi], rows[1][xi], rows[2][xi])):
            u[layer, 4 * xi + nu, part] = value.astype(BF)


def tile_kernel(
    feat, top, bottom, edge, w_red, w_spa, w_exp, w_first, w_rest, w_log, w_br, w_bh, w_bs, w_bp,
    anchor, dest,
    sec, lg, sc,
    xe, inr, cat, xs, mv, redf, avg, pick, pick_side, ma, mb, prod, box_t,
    v_red, v_spa, v_exp, v_first, v_rest, v_fil, v_br, v_bh, v_bs,
    sems,
):
    row_at = lax.axis_index("ty")
    col_at = lax.axis_index("tx")
    rows_of = lax.axis_size("ty")
    cols_of = lax.axis_size("tx")

    copies = [
        pltpu.make_async_copy(feat, xe.at[2:34, 0:TILE], sems.at[0]),
        pltpu.make_async_copy(top, xe.at[0:2], sems.at[1]),
        pltpu.make_async_copy(bottom, xe.at[34:36], sems.at[2]),
        pltpu.make_async_copy(edge, xe.at[2:34, TILE:WIDE], sems.at[3]),
        pltpu.make_async_copy(w_red, v_red, sems.at[4]),
        pltpu.make_async_copy(w_spa, v_spa, sems.at[5]),
        pltpu.make_async_copy(w_exp, v_exp, sems.at[6]),
        pltpu.make_async_copy(w_first, v_first, sems.at[7]),
        pltpu.make_async_copy(w_br, v_br, sems.at[8]),
        pltpu.make_async_copy(w_rest, v_rest, sems.at[9]),
        pltpu.make_async_copy(w_bh, v_bh, sems.at[10]),
        pltpu.make_async_copy(w_bs, v_bs, sems.at[11]),
    ]
    for copy in copies[:7]:
        copy.start()

    for j in range(3):
        xs[j, 0, :, :] = jnp.zeros((TILE, CH), BF)
        xs[j, TILE + 1, :, :] = jnp.zeros((TILE, CH), BF)
    for v in range(9):
        mv[v, TILE : TILE + 2, :, :] = jnp.zeros((2, TILE, MASK_CH), BF)
    redf[TILE * TILE : TILE * TILE + 40, :] = jnp.zeros((40, BOX_CH), F32)
    line = jnp.zeros((8, SLOTS, MASK_CH), BF)
    for ref in (ma, mb):
        for parity in range(2):
            ref[0, parity] = line
            ref[15, parity] = line
        for r in range(1, 15):
            ref[r, 0, 0] = line[0]
            ref[r, 1, 7] = line[0]

    def column(row):
        return jnp.broadcast_to(row.astype(F32), (SLOTS, SLOTS)).T[:, :1].astype(jnp.int32)

    used = dest[...] >= 0
    used_column = column(used)
    at = column(anchor[0:1] * TILE + anchor[1:2])
    log_w = jnp.broadcast_to(w_log[...].reshape(1, MASK_CH).astype(F32), (128, MASK_CH)).T.astype(BF)
    lanes = lax.broadcasted_iota(jnp.int32, (SLOTS, SPAN), 1) - at
    for k, c in enumerate([*range(0, CROP, 2), *range(1, CROP, 2)]):
        pick[k] = jnp.where(lanes == c, 1.0, 0.0).astype(BF)
    lanes = lax.broadcasted_iota(jnp.int32, (SLOTS, TILE * TILE), 1) - at
    for side, c in enumerate((0, CROP - 1)):
        for r in range(1, CROP - 1):
            pick_side[side, r - 1] = jnp.where(lanes == r * TILE + c, 1.0, 0.0).astype(BF)

    for copy in copies[:7]:
        copy.wait()
    for copy in copies[7:]:
        copy.start()

    first_row, last_row = row_at == 0, row_at == rows_of - 1
    first_col, last_col = col_at == 0, col_at == cols_of - 1

    for b in range(2):
        for r in range(0, TALL, 4):
            x = xe[r : r + 4].reshape(4 * WIDE, CH)
            inr[r : r + 4] = jnp.maximum(mm(x, v_red[b]), 0.0).reshape(4, WIDE, INNER)
        inr[0:2] = jnp.where(first_row, 0.0, inr[0:2])
        inr[34:36] = jnp.where(last_row, 0.0, inr[34:36])
        inr[:, 40:48] = jnp.where(first_col, 0.0, inr[:, 40:48])
        inr[:, 32:40] = jnp.where(last_col, 0.0, inr[:, 32:40])

        for r in range(TALL):
            line = inr[r]
            cat[r, :, :INNER] = pltpu.roll(line, 1, 0).astype(BF)
            cat[r, :, INNER : 2 * INNER] = line.astype(BF)
            cat[r, :, 2 * INNER :] = pltpu.roll(line, WIDE - 1, 0).astype(BF)

        for r, per in ((1, 7), (8, 7), (15, 7), (22, 7), (29, 6)) if b == 0 else (
            (2, 8), (10, 8), (18, 8), (26, 8)
        ):
            lhs = jnp.concatenate([cat[r + i - 1 : r + i - 1 + per] for i in range(3)], axis=2)
            h = jnp.maximum(mm(lhs.reshape(per * WIDE, 9 * INNER), v_spa[b]), 0.0).astype(BF)
            y = mm(h, v_exp[b]) + xe[r : r + per].reshape(per * WIDE, CH).astype(F32)
            y = jnp.maximum(y, 0.0).astype(BF).reshape(per, WIDE, CH)
            if b == 0:
                xe[r : r + per] = y
            else:
                y = y[:, :TILE]
                xs[1, r - 1 : r - 1 + per] = y
                flat = y.reshape(per * TILE, CH).astype(F32)
                for j, shift in ((0, 1), (2, per * TILE - 1)):
                    moved = pltpu.roll(flat, shift, 0).astype(BF)
                    xs[j, r - 1 : r - 1 + per] = moved.reshape(per, TILE, CH)

    out_copy = pltpu.make_async_copy(xs.at[1, 1 : TILE + 1], sec, sems.at[12])
    out_copy.start()
    copies[7].wait()
    copies[8].wait()

    def stem_rows(k, _):
        r = k * 8
        for i in range(3):
            for j in range(3):
                lhs = xs[j, pl.ds(r + i, 8)].reshape(8 * TILE, CH)
                prod[3 * i + j, : 8 * TILE] = mm(lhs, v_first[3 * i + j])
        sums = []
        for i in range(3):
            t0, t1, t2 = (prod[3 * i + j, : 8 * TILE] for j in range(3))
            right = t0 + t1
            sums.append((t1 + t2, right + t2, right))
        for cv in range(3):
            a0, a1, a2 = sums[0][cv], sums[1][cv], sums[2][cv]
            low = a0 + a1
            for rv, value in enumerate((a1 + a2, low + a2, low)):
                value = jnp.maximum(value, 0.0).astype(BF).reshape(8, TILE, MASK_CH)
                mv[3 * rv + cv, pl.ds(r, 8)] = value
        red = mm(xs[1, pl.ds(r + 1, 8)].reshape(8 * TILE, CH), v_br[...])
        redf[pl.ds(pl.multiple_of(r * TILE, 8), 8 * TILE), :] = red
        return 0

    for k in range(4):
        stem_rows(k, 0)

    def average_rows(k, _):
        here = pl.multiple_of(k * 4 * TILE, 8)
        block = redf[pl.ds(here, 5 * TILE + 8), :]
        pair = block[: 5 * TILE] + block[1 : 5 * TILE + 1]
        quad = (pair[: 4 * TILE] + pair[TILE:]) * 0.25
        avg[pl.ds(k * 4, 4)] = quad.astype(BF).reshape(4, TILE, BOX_CH)
        return 0

    lax.fori_loop(0, 8, average_rows, 0, unroll=True)

    inside = CROP - 2

    def choose(picker, source):
        return mm(picker, source).astype(BF)

    def table(v, r):
        return mv[v, pl.ds(r, WINDOW)].reshape(SPAN, MASK_CH)

    last = CROP - 1
    half = CROP // 2

    def gather_inside(r, v):
        got = choose(pick[1:last].reshape(inside * SLOTS, SPAN), table(v, r))
        got = got.reshape(2, half - 1, SLOTS, MASK_CH)
        ma[r + 1, 1, 1:half] = got[0]
        ma[r + 1, 0, 1:half] = got[1]

    copies[9].wait()
    for r in range(1, last):
        gather_inside(r, 4)
        quarter = (r - 1) % 4 * (MASK_CH // 4)
        filter_weights(v_rest, v_fil, (r - 1) // 4, slice(quarter, quarter + MASK_CH // 4))
    for r, v in ((0, 1), (last, 7)):
        gather_inside(r, v)
        ma[r + 1, 1, 0] = choose(pick[0], table(v - 1, r))
        ma[r + 1, 0, half] = choose(pick[last], table(v + 1, r))
    for side, v in ((0, 3), (1, 5)):
        got = choose(
            pick_side[side].reshape(inside * SLOTS, TILE * TILE),
            mv[v, 0:TILE].reshape(TILE * TILE, MASK_CH),
        )
        ma[2:CROP, 1 - side, side * half] = got.reshape(inside, SLOTS, MASK_CH)

    for copy in copies[10:12]:
        copy.wait()

    def filtered(layer, source, group):
        tiles = []
        for t in group:
            d0, d1, d2, d3 = (source[2 * t + k] for k in range(4))
            tile = []
            for w in (d0 - d2, d1 + d2, d2 - d1, d1 - d3):
                even, odd = w[0], w[1]
                e0, e1, o0, o1 = even[:half], even[1:], odd[:half], odd[1:]
                tile += [e0 - e1, o0 + e1, e1 - o0, o0 - o1]
            tiles.append(tile)
        size = half * SLOTS
        for k in range(16):
            lhs = jnp.concatenate([tile[k].reshape(size, MASK_CH) for tile in tiles], axis=0)
            prod[k, : len(group) * size] = mm(lhs, v_fil[layer, k])
        for n, t in enumerate(group):
            lines = []
            for xi in range(4):
                m0, m1, m2, m3 = (
                    prod[4 * xi + nu, n * size : (n + 1) * size] for nu in range(4)
                )
                lines.append((m0 + m1 + m2, m1 - m2 - m3))
            for b in range(2):
                y0, y1, y2, y3 = (lines[xi][b] for xi in range(4))
                for a, y in enumerate((y0 + y1 + y2, y1 - y2 - y3)):
                    yield t, a, b, jnp.maximum(y, 0.0).astype(BF)

    cell_lane = lax.broadcasted_iota(jnp.int32, (SLOTS, 128), 1)
    logits = [jnp.zeros((SLOTS, 128), F32)] * 2
    total = jnp.zeros((SLOTS, FC), F32)
    even = pick[0:half].reshape(half * SLOTS, SPAN)

    for layer in range(3):
        source, target = (ma, mb) if layer % 2 == 0 else (mb, ma)
        for group in GROUPS:
            final = []
            for t, a, b, act in filtered(layer, source, group):
                if layer < 2:
                    act = act.reshape(half, SLOTS, MASK_CH)
                    target[2 * t + a + 1, 1 - b, b : b + half] = act
                    continue
                final.append(act)
                if len(final) < 4:
                    continue
                got = mm(jnp.concatenate(final, axis=0), log_w)
                final = []
                for k in range(4 * half):
                    u = k % half
                    b, a = divmod(k // half, 2)
                    h, cell = divmod((2 * t + a) * CROP + 2 * u + b, 128)
                    part = got[k * SLOTS : (k + 1) * SLOTS]
                    logits[h] = jnp.where(cell_lane == cell, part, logits[h])
            for t in group:
                if layer == 0:
                    got = choose(even, avg[2 * t : 2 * t + WINDOW].reshape(SPAN, BOX_CH))
                    for u in range(half):
                        part = got[u * SLOTS : (u + 1) * SLOTS]
                        box_t[t, :, u * BOX_CH : (u + 1) * BOX_CH] = part
                if layer == 1:
                    part = v_bh[t * half * BOX_CH : (t + 1) * half * BOX_CH, :]
                    total = total + mm(box_t[t], part)
    logits = jnp.where(used_column > 0, jnp.concatenate(logits, axis=1), 0.0)
    lg[0, 0] = logits[:, : CROP * CROP]

    first_box = jnp.maximum(total, 0.0).astype(BF)
    next_box = jnp.maximum(mm(first_box, v_bs[...]), 0.0).astype(BF)
    scores = lax.dot_general(
        w_bp[...], next_box, (((1,), (1,)), ((), ())), preferred_element_type=F32
    )
    scores = jnp.where(used, scores, 0.0)
    for k in range(5):
        sc[0, k] = scores[k : k + 1]
    out_copy.wait()


def exchange(features):
    rows, cols = lax.axis_size("ty"), lax.axis_size("tx")

    def send(part, down, right):
        pairs = [
            (r * cols + c, (r + down) % rows * cols + (c + right) % cols)
            for r in range(rows)
            for c in range(cols)
        ]
        return lax.ppermute(part, ("ty", "tx"), pairs)

    left = send(features[:, -2:], 0, 1)
    right = send(features[:, :2], 0, -1)
    edge = jnp.pad(left, ((0, 0), (14, 0), (0, 0))) + jnp.pad(right, ((0, 0), (0, 14), (0, 0)))
    top = send(jnp.concatenate([features[-2:], edge[-2:]], axis=1), 1, 0)
    bottom = send(jnp.concatenate([features[:2], edge[:2]], axis=1), -1, 0)
    return top, bottom, edge


def on_device(
    features, block_reduce, block_spatial, block_expand, mask_first, mask_rest, mask_logit,
    box_reduce, box_hidden, box_second, box_predict, roi_anchor, roi_dest, roi_slot,
):
    top, bottom, edge = exchange(features)
    hbm = pl.BlockSpec(memory_space=pl.ANY)
    vmem = pl.BlockSpec(memory_space=pltpu.VMEM)
    sec, lg, sc = pl.pallas_call(
        tile_kernel,
        out_shape=(
            jax.ShapeDtypeStruct((TILE, TILE, CH), BF),
            jax.ShapeDtypeStruct((1, 1, SLOTS, CROP * CROP), F32),
            jax.ShapeDtypeStruct((1, 5, 1, SLOTS), F32),
        ),
        in_specs=[hbm] * 9 + [vmem] + [hbm] * 3 + [vmem, vmem, vmem],
        out_specs=(hbm, vmem, vmem),
        scratch_shapes=[
            pltpu.VMEM((TALL, WIDE, CH), BF),
            pltpu.VMEM((TALL, WIDE, INNER), F32),
            pltpu.VMEM((TALL, WIDE, 3 * INNER), BF),
            pltpu.VMEM((3, TILE + 2, TILE, CH), BF),
            pltpu.VMEM((9, TILE + 2, TILE, MASK_CH), BF),
            pltpu.VMEM((TILE * TILE + 40, BOX_CH), F32),
            pltpu.VMEM((TILE, TILE, BOX_CH), BF),
            pltpu.VMEM((CROP, SLOTS, SPAN), BF),
            pltpu.VMEM((2, CROP - 2, SLOTS, TILE * TILE), BF),
            pltpu.VMEM((16, 2, 8, SLOTS, MASK_CH), BF),
            pltpu.VMEM((16, 2, 8, SLOTS, MASK_CH), BF),
            pltpu.VMEM((16, 14 * SLOTS, MASK_CH), F32),
            pltpu.VMEM((CROP // 2, SLOTS, CROP // 2 * BOX_CH), BF),
            pltpu.VMEM((2, CH, INNER), BF),
            pltpu.VMEM((2, 9 * INNER, INNER), BF),
            pltpu.VMEM((2, INNER, CH), BF),
            pltpu.VMEM((9, CH, MASK_CH), BF),
            pltpu.VMEM((3, 9, MASK_CH, MASK_CH), BF),
            pltpu.VMEM((3, 16, MASK_CH, MASK_CH), BF),
            pltpu.VMEM((CH, BOX_CH), BF),
            pltpu.VMEM(((CROP // 2) ** 2 * BOX_CH, FC), BF),
            pltpu.VMEM((FC, FC), BF),
            pltpu.SemaphoreType.DMA((13,)),
        ],
        compiler_params=pltpu.CompilerParams(vmem_limit_bytes=62 * 1024 * 1024),
        name="tile_heads",
    )(
        features, top, bottom, edge,
        block_reduce, block_spatial.reshape(2, 9 * INNER, INNER), block_expand,
        mask_first, mask_rest, mask_logit,
        box_reduce, box_hidden, box_second, box_predict.T, roi_anchor[0, 0].T, roi_dest[0],
    )
    return sec, lg, sc.transpose(0, 2, 3, 1)


def solution(mesh):
    whole = P()
    in_specs = (P("ty", "tx", None),) + (whole,) * 10 + (
        P("ty", "tx", None, None), P("ty", "tx", None), P("ty", "tx", None),
    )
    out_specs = (P("ty", "tx", None), P("ty", "tx", None, None), P("ty", "tx", None, None))
    return jax.shard_map(
        on_device, mesh=mesh, in_specs=in_specs, out_specs=out_specs, check_vma=False
    )
```

```python
import jax
import jax.numpy as jnp
from jax import lax
from jax.experimental import pallas as pl
from jax.experimental.pallas import tpu as pltpu
from jax.sharding import PartitionSpec as P

CROP = 14
TILE = 32
WIDE = 48
TALL = 36
CH = 512
INNER = 128
MASK_CH = 256
BOX_CH = 128
FC = 1024
SLOTS = 32
WINDOW = 20
GROUPS = ((0, 1), (2, 3), (4, 5), (6,))
SPAN = WINDOW * TILE
BF = jnp.bfloat16
F32 = jnp.float32


def mm(a, b):
    return jnp.dot(a, b, preferred_element_type=F32)


def spread(a, b, c):
    even, odd = (a + c) * 0.5, b * 0.5
    return a, even + odd, even - odd, c


def filter_weights(w, u, layer, part):
    taps = [w[layer, k, part].astype(F32) for k in range(9)]
    rows = [spread(taps[j], taps[3 + j], taps[6 + j]) for j in range(3)]
    for xi in range(4):
        for nu, value in enumerate(spread(rows[0][xi], rows[1][xi], rows[2][xi])):
            u[layer, 4 * xi + nu, part] = value.astype(BF)


def tile_kernel(
    feat, top, bottom, edge, w_red, w_spa, w_exp, w_first, w_rest, w_log, w_br, w_bh, w_bs, w_bp,
    anchor, dest,
    sec, lg, sc,
    xe, inr, cat, xs, mv, redf, avg, pick, pick_side, ma, mb, prod, box_t,
    v_red, v_spa, v_exp, v_first, v_rest, v_fil, v_br, v_bh, v_bs,
    sems,
):
    row_at = lax.axis_index("ty")
    col_at = lax.axis_index("tx")
    rows_of = lax.axis_size("ty")
    cols_of = lax.axis_size("tx")

    copies = [
        pltpu.make_async_copy(feat, xe.at[2:34, 0:TILE], sems.at[0]),
        pltpu.make_async_copy(top, xe.at[0:2], sems.at[1]),
        pltpu.make_async_copy(bottom, xe.at[34:36], sems.at[2]),
        pltpu.make_async_copy(edge, xe.at[2:34, TILE:WIDE], sems.at[3]),
        pltpu.make_async_copy(w_red, v_red, sems.at[4]),
        pltpu.make_async_copy(w_spa, v_spa, sems.at[5]),
        pltpu.make_async_copy(w_exp, v_exp, sems.at[6]),
        pltpu.make_async_copy(w_first, v_first, sems.at[7]),
        pltpu.make_async_copy(w_br, v_br, sems.at[8]),
        pltpu.make_async_copy(w_rest, v_rest, sems.at[9]),
        pltpu.make_async_copy(w_bh, v_bh, sems.at[10]),
        pltpu.make_async_copy(w_bs, v_bs, sems.at[11]),
    ]
    for copy in copies[:7]:
        copy.start()

    for j in range(3):
        xs[j, 0, :, :] = jnp.zeros((TILE, CH), BF)
        xs[j, TILE + 1, :, :] = jnp.zeros((TILE, CH), BF)
    for v in range(9):
        mv[v, TILE : TILE + 2, :, :] = jnp.zeros((2, TILE, MASK_CH), BF)
    redf[TILE * TILE : TILE * TILE + 40, :] = jnp.zeros((40, BOX_CH), F32)
    line = jnp.zeros((8, SLOTS, MASK_CH), BF)
    for ref in (ma, mb):
        for parity in range(2):
            ref[0, parity] = line
            ref[15, parity] = line
        for r in range(1, 15):
            ref[r, 0, 0] = line[0]
            ref[r, 1, 7] = line[0]

    def column(row):
        return jnp.broadcast_to(row.astype(F32), (SLOTS, SLOTS)).T[:, :1].astype(jnp.int32)

    used = dest[...] >= 0
    used_column = column(used)
    at = column(anchor[0:1] * TILE + anchor[1:2])
    log_w = jnp.broadcast_to(w_log[...].reshape(1, MASK_CH).astype(F32), (128, MASK_CH)).T.astype(BF)
    lanes = lax.broadcasted_iota(jnp.int32, (SLOTS, SPAN), 1) - at
    for k, c in enumerate([*range(0, CROP, 2), *range(1, CROP, 2)]):
        pick[k] = jnp.where(lanes == c, 1.0, 0.0).astype(BF)
    lanes = lax.broadcasted_iota(jnp.int32, (SLOTS, TILE * TILE), 1) - at
    for side, c in enumerate((0, CROP - 1)):
        for r in range(1, CROP - 1):
            pick_side[side, r - 1] = jnp.where(lanes == r * TILE + c, 1.0, 0.0).astype(BF)

    for copy in copies[:7]:
        copy.wait()
    for copy in copies[7:]:
        copy.start()

    first_row, last_row = row_at == 0, row_at == rows_of - 1
    first_col, last_col = col_at == 0, col_at == cols_of - 1

    for b in range(2):
        for r in range(0, TALL, 4):
            x = xe[r : r + 4].reshape(4 * WIDE, CH)
            inr[r : r + 4] = jnp.maximum(mm(x, v_red[b]), 0.0).reshape(4, WIDE, INNER)
        inr[0:2] = jnp.where(first_row, 0.0, inr[0:2])
        inr[34:36] = jnp.where(last_row, 0.0, inr[34:36])
        inr[:, 40:48] = jnp.where(first_col, 0.0, inr[:, 40:48])
        inr[:, 32:40] = jnp.where(last_col, 0.0, inr[:, 32:40])

        for r in range(TALL):
            line = inr[r]
            cat[r, :, :INNER] = pltpu.roll(line, 1, 0).astype(BF)
            cat[r, :, INNER : 2 * INNER] = line.astype(BF)
            cat[r, :, 2 * INNER :] = pltpu.roll(line, WIDE - 1, 0).astype(BF)

        for r, per in ((1, 7), (8, 7), (15, 7), (22, 7), (29, 6)) if b == 0 else (
            (2, 8), (10, 8), (18, 8), (26, 8)
        ):
            lhs = jnp.concatenate([cat[r + i - 1 : r + i - 1 + per] for i in range(3)], axis=2)
            h = jnp.maximum(mm(lhs.reshape(per * WIDE, 9 * INNER), v_spa[b]), 0.0).astype(BF)
            y = mm(h, v_exp[b]) + xe[r : r + per].reshape(per * WIDE, CH).astype(F32)
            y = jnp.maximum(y, 0.0).astype(BF).reshape(per, WIDE, CH)
            if b == 0:
                xe[r : r + per] = y
            else:
                y = y[:, :TILE]
                xs[1, r - 1 : r - 1 + per] = y
                flat = y.reshape(per * TILE, CH).astype(F32)
                for j, shift in ((0, 1), (2, per * TILE - 1)):
                    moved = pltpu.roll(flat, shift, 0).astype(BF)
                    xs[j, r - 1 : r - 1 + per] = moved.reshape(per, TILE, CH)

    out_copy = pltpu.make_async_copy(xs.at[1, 1 : TILE + 1], sec, sems.at[12])
    out_copy.start()
    copies[7].wait()
    copies[8].wait()

    def stem_rows(k, _):
        r = k * 8
        for i in range(3):
            for j in range(3):
                lhs = xs[j, pl.ds(r + i, 8)].reshape(8 * TILE, CH)
                prod[3 * i + j, : 8 * TILE] = mm(lhs, v_first[3 * i + j])
        sums = []
        for i in range(3):
            t0, t1, t2 = (prod[3 * i + j, : 8 * TILE] for j in range(3))
            right = t0 + t1
            sums.append((t1 + t2, right + t2, right))
        for cv in range(3):
            a0, a1, a2 = sums[0][cv], sums[1][cv], sums[2][cv]
            low = a0 + a1
            for rv, value in enumerate((a1 + a2, low + a2, low)):
                value = jnp.maximum(value, 0.0).astype(BF).reshape(8, TILE, MASK_CH)
                mv[3 * rv + cv, pl.ds(r, 8)] = value
        red = mm(xs[1, pl.ds(r + 1, 8)].reshape(8 * TILE, CH), v_br[...])
        redf[pl.ds(pl.multiple_of(r * TILE, 8), 8 * TILE), :] = red
        return 0

    for k in range(4):
        stem_rows(k, 0)

    def average_rows(k, _):
        here = pl.multiple_of(k * 4 * TILE, 8)
        block = redf[pl.ds(here, 5 * TILE + 8), :]
        pair = block[: 5 * TILE] + block[1 : 5 * TILE + 1]
        quad = (pair[: 4 * TILE] + pair[TILE:]) * 0.25
        avg[pl.ds(k * 4, 4)] = quad.astype(BF).reshape(4, TILE, BOX_CH)
        return 0

    lax.fori_loop(0, 8, average_rows, 0, unroll=True)

    inside = CROP - 2

    def choose(picker, source):
        return mm(picker, source).astype(BF)

    def table(v, r):
        return mv[v, pl.ds(r, WINDOW)].reshape(SPAN, MASK_CH)

    last = CROP - 1
    half = CROP // 2

    def gather_inside(r, v):
        got = choose(pick[1:last].reshape(inside * SLOTS, SPAN), table(v, r))
        got = got.reshape(2, half - 1, SLOTS, MASK_CH)
        ma[r + 1, 1, 1:half] = got[0]
        ma[r + 1, 0, 1:half] = got[1]

    copies[9].wait()
    for r in range(1, last):
        gather_inside(r, 4)
        quarter = (r - 1) % 4 * (MASK_CH // 4)
        filter_weights(v_rest, v_fil, (r - 1) // 4, slice(quarter, quarter + MASK_CH // 4))
    for r, v in ((0, 1), (last, 7)):
        gather_inside(r, v)
        ma[r + 1, 1, 0] = choose(pick[0], table(v - 1, r))
        ma[r + 1, 0, half] = choose(pick[last], table(v + 1, r))
    for side, v in ((0, 3), (1, 5)):
        got = choose(
            pick_side[side].reshape(inside * SLOTS, TILE * TILE),
            mv[v, 0:TILE].reshape(TILE * TILE, MASK_CH),
        )
        ma[2:CROP, 1 - side, side * half] = got.reshape(inside, SLOTS, MASK_CH)

    for copy in copies[10:12]:
        copy.wait()

    def filtered(layer, source, group):
        tiles = []
        for t in group:
            d0, d1, d2, d3 = (source[2 * t + k] for k in range(4))
            tile = []
            for w in (d0 - d2, d1 + d2, d2 - d1, d1 - d3):
                even, odd = w[0], w[1]
                e0, e1, o0, o1 = even[:half], even[1:], odd[:half], odd[1:]
                tile += [e0 - e1, o0 + e1, e1 - o0, o0 - o1]
            tiles.append(tile)
        size = half * SLOTS
        for k in range(16):
            lhs = jnp.concatenate([tile[k].reshape(size, MASK_CH) for tile in tiles], axis=0)
            prod[k, : len(group) * size] = mm(lhs, v_fil[layer, k])
        for n, t in enumerate(group):
            lines = []
            for xi in range(4):
                m0, m1, m2, m3 = (
                    prod[4 * xi + nu, n * size : (n + 1) * size] for nu in range(4)
                )
                lines.append((m0 + m1 + m2, m1 - m2 - m3))
            for b in range(2):
                y0, y1, y2, y3 = (lines[xi][b] for xi in range(4))
                for a, y in enumerate((y0 + y1 + y2, y1 - y2 - y3)):
                    yield t, a, b, jnp.maximum(y, 0.0).astype(BF)

    cell_lane = lax.broadcasted_iota(jnp.int32, (SLOTS, 128), 1)
    logits = [jnp.zeros((SLOTS, 128), F32)] * 2
    total = jnp.zeros((SLOTS, FC), F32)
    even = pick[0:half].reshape(half * SLOTS, SPAN)

    for layer in range(3):
        source, target = (ma, mb) if layer % 2 == 0 else (mb, ma)
        for group in GROUPS:
            final = []
            for t, a, b, act in filtered(layer, source, group):
                if layer < 2:
                    act = act.reshape(half, SLOTS, MASK_CH)
                    target[2 * t + a + 1, 1 - b, b : b + half] = act
                    continue
                final.append(act)
                if len(final) < 4:
                    continue
                got = mm(jnp.concatenate(final, axis=0), log_w)
                final = []
                for k in range(4 * half):
                    u = k % half
                    b, a = divmod(k // half, 2)
                    h, cell = divmod((2 * t + a) * CROP + 2 * u + b, 128)
                    part = got[k * SLOTS : (k + 1) * SLOTS]
                    logits[h] = jnp.where(cell_lane == cell, part, logits[h])
            for t in group:
                if layer == 0:
                    got = choose(even, avg[2 * t : 2 * t + WINDOW].reshape(SPAN, BOX_CH))
                    for u in range(half):
                        part = got[u * SLOTS : (u + 1) * SLOTS]
                        box_t[t, :, u * BOX_CH : (u + 1) * BOX_CH] = part
                if layer == 1:
                    part = v_bh[t * half * BOX_CH : (t + 1) * half * BOX_CH, :]
                    total = total + mm(box_t[t], part)
    logits = jnp.where(used_column > 0, jnp.concatenate(logits, axis=1), 0.0)
    lg[0, 0] = logits[:, : CROP * CROP]

    first_box = jnp.maximum(total, 0.0).astype(BF)
    next_box = jnp.maximum(mm(first_box, v_bs[...]), 0.0).astype(BF)
    scores = lax.dot_general(
        w_bp[...], next_box, (((1,), (1,)), ((), ())), preferred_element_type=F32
    )
    scores = jnp.where(used, scores, 0.0)
    for k in range(5):
        sc[0, k] = scores[k : k + 1]
    out_copy.wait()


def exchange(features):
    rows, cols = lax.axis_size("ty"), lax.axis_size("tx")

    def send(part, down, right):
        pairs = [
            (r * cols + c, (r + down) % rows * cols + c + right)
            for r in range(rows)
            for c in range(cols)
            if 0 <= c + right < cols
        ]
        return lax.ppermute(part, ("ty", "tx"), pairs)

    left = send(features[:, -2:], 0, 1)
    right = send(features[:, :2], 0, -1)
    edge = jnp.pad(left, ((0, 0), (14, 0), (0, 0))) + jnp.pad(right, ((0, 0), (0, 14), (0, 0)))
    top = send(jnp.concatenate([features[-2:], edge[-2:]], axis=1), 1, 0)
    bottom = send(jnp.concatenate([features[:2], edge[:2]], axis=1), -1, 0)
    return top, bottom, edge


def on_device(
    features, block_reduce, block_spatial, block_expand, mask_first, mask_rest, mask_logit,
    box_reduce, box_hidden, box_second, box_predict, roi_anchor, roi_dest, roi_slot,
):
    top, bottom, edge = exchange(features)
    hbm = pl.BlockSpec(memory_space=pl.ANY)
    vmem = pl.BlockSpec(memory_space=pltpu.VMEM)
    sec, lg, sc = pl.pallas_call(
        tile_kernel,
        out_shape=(
            jax.ShapeDtypeStruct((TILE, TILE, CH), BF),
            jax.ShapeDtypeStruct((1, 1, SLOTS, CROP * CROP), F32),
            jax.ShapeDtypeStruct((1, 5, 1, SLOTS), F32),
        ),
        in_specs=[hbm] * 9 + [vmem] + [hbm] * 3 + [vmem, vmem, vmem],
        out_specs=(hbm, vmem, vmem),
        scratch_shapes=[
            pltpu.VMEM((TALL, WIDE, CH), BF),
            pltpu.VMEM((TALL, WIDE, INNER), F32),
            pltpu.VMEM((TALL, WIDE, 3 * INNER), BF),
            pltpu.VMEM((3, TILE + 2, TILE, CH), BF),
            pltpu.VMEM((9, TILE + 2, TILE, MASK_CH), BF),
            pltpu.VMEM((TILE * TILE + 40, BOX_CH), F32),
            pltpu.VMEM((TILE, TILE, BOX_CH), BF),
            pltpu.VMEM((CROP, SLOTS, SPAN), BF),
            pltpu.VMEM((2, CROP - 2, SLOTS, TILE * TILE), BF),
            pltpu.VMEM((16, 2, 8, SLOTS, MASK_CH), BF),
            pltpu.VMEM((16, 2, 8, SLOTS, MASK_CH), BF),
            pltpu.VMEM((16, 14 * SLOTS, MASK_CH), F32),
            pltpu.VMEM((CROP // 2, SLOTS, CROP // 2 * BOX_CH), BF),
            pltpu.VMEM((2, CH, INNER), BF),
            pltpu.VMEM((2, 9 * INNER, INNER), BF),
            pltpu.VMEM((2, INNER, CH), BF),
            pltpu.VMEM((9, CH, MASK_CH), BF),
            pltpu.VMEM((3, 9, MASK_CH, MASK_CH), BF),
            pltpu.VMEM((3, 16, MASK_CH, MASK_CH), BF),
            pltpu.VMEM((CH, BOX_CH), BF),
            pltpu.VMEM(((CROP // 2) ** 2 * BOX_CH, FC), BF),
            pltpu.VMEM((FC, FC), BF),
            pltpu.SemaphoreType.DMA((13,)),
        ],
        compiler_params=pltpu.CompilerParams(vmem_limit_bytes=62 * 1024 * 1024),
        name="tile_heads",
    )(
        features, top, bottom, edge,
        block_reduce, block_spatial.reshape(2, 9 * INNER, INNER), block_expand,
        mask_first, mask_rest, mask_logit,
        box_reduce, box_hidden, box_second, box_predict.T, roi_anchor[0, 0].T, roi_dest[0],
    )
    return sec, lg, sc.transpose(0, 2, 3, 1)


def solution(mesh):
    whole = P()
    in_specs = (P("ty", "tx", None),) + (whole,) * 10 + (
        P("ty", "tx", None, None), P("ty", "tx", None), P("ty", "tx", None),
    )
    out_specs = (P("ty", "tx", None), P("ty", "tx", None, None), P("ty", "tx", None, None))
    return jax.shard_map(
        on_device, mesh=mesh, in_specs=in_specs, out_specs=out_specs, check_vma=False
    )
```

```python
import jax
import jax.numpy as jnp
from jax import lax
from jax.experimental import pallas as pl
from jax.experimental.pallas import tpu as pltpu
from jax.sharding import PartitionSpec as P

CROP = 14
TILE = 32
WIDE = 48
TALL = 36
CH = 512
INNER = 128
MASK_CH = 256
BOX_CH = 128
FC = 1024
SLOTS = 32
WINDOW = 20
GROUPS = ((0, 1), (2, 3), (4, 5), (6,))
SPAN = WINDOW * TILE
BF = jnp.bfloat16
F32 = jnp.float32


def mm(a, b):
    return jnp.dot(a, b, preferred_element_type=F32)


def spread(a, b, c):
    even, odd = (a + c) * 0.5, b * 0.5
    return a, even + odd, even - odd, c


def filter_weights(w, u, layer, part):
    taps = [w[layer, k, part].astype(F32) for k in range(9)]
    rows = [spread(taps[j], taps[3 + j], taps[6 + j]) for j in range(3)]
    for xi in range(4):
        for nu, value in enumerate(spread(rows[0][xi], rows[1][xi], rows[2][xi])):
            u[layer, 4 * xi + nu, part] = value.astype(BF)


def tile_kernel(
    feat, top, bottom, edge, w_red, w_spa, w_exp, w_first, w_rest, w_log, w_br, w_bh, w_bs, w_bp,
    anchor, dest,
    sec, lg, sc,
    xe, inr, cat, xs, mv, redf, avg, pick, pick_side, ma, mb, prod, box_t,
    v_red, v_spa, v_exp, v_first, v_rest, v_fil, v_br, v_bh, v_bs,
    sems,
):
    row_at = lax.axis_index("ty")
    col_at = lax.axis_index("tx")
    rows_of = lax.axis_size("ty")
    cols_of = lax.axis_size("tx")

    copies = [
        pltpu.make_async_copy(feat, xe.at[2:34, 0:TILE], sems.at[0]),
        pltpu.make_async_copy(top, xe.at[0:2], sems.at[1]),
        pltpu.make_async_copy(bottom, xe.at[34:36], sems.at[2]),
        pltpu.make_async_copy(edge, xe.at[2:34, TILE:WIDE], sems.at[3]),
        pltpu.make_async_copy(w_red, v_red, sems.at[4]),
        pltpu.make_async_copy(w_spa, v_spa, sems.at[5]),
        pltpu.make_async_copy(w_exp, v_exp, sems.at[6]),
        pltpu.make_async_copy(w_first, v_first, sems.at[7]),
        pltpu.make_async_copy(w_br, v_br, sems.at[8]),
        pltpu.make_async_copy(w_rest, v_rest, sems.at[9]),
        pltpu.make_async_copy(w_bh, v_bh, sems.at[10]),
        pltpu.make_async_copy(w_bs, v_bs, sems.at[11]),
    ]
    for copy in copies[:7]:
        copy.start()

    for j in range(3):
        xs[j, 0, :, :] = jnp.zeros((TILE, CH), BF)
        xs[j, TILE + 1, :, :] = jnp.zeros((TILE, CH), BF)
    for v in range(9):
        mv[v, TILE : TILE + 2, :, :] = jnp.zeros((2, TILE, MASK_CH), BF)
    redf[TILE * TILE : TILE * TILE + 40, :] = jnp.zeros((40, BOX_CH), F32)
    line = jnp.zeros((8, SLOTS, MASK_CH), BF)
    for ref in (ma, mb):
        for parity in range(2):
            ref[0, parity] = line
            ref[15, parity] = line
        for r in range(1, 15):
            ref[r, 0, 0] = line[0]
            ref[r, 1, 7] = line[0]

    def column(row):
        return jnp.broadcast_to(row.astype(F32), (SLOTS, SLOTS)).T[:, :1].astype(jnp.int32)

    used = dest[...] >= 0
    used_column = column(used)
    at = column(anchor[0:1] * TILE + anchor[1:2])
    log_w = jnp.broadcast_to(w_log[...].reshape(1, MASK_CH).astype(F32), (128, MASK_CH)).T.astype(BF)
    lanes = lax.broadcasted_iota(jnp.int32, (SLOTS, SPAN), 1) - at
    for k, c in enumerate([*range(0, CROP, 2), *range(1, CROP, 2)]):
        pick[k] = jnp.where(lanes == c, 1.0, 0.0).astype(BF)
    lanes = lax.broadcasted_iota(jnp.int32, (SLOTS, TILE * TILE), 1) - at
    for side, c in enumerate((0, CROP - 1)):
        for r in range(1, CROP - 1):
            pick_side[side, r - 1] = jnp.where(lanes == r * TILE + c, 1.0, 0.0).astype(BF)

    for copy in copies[:7]:
        copy.wait()
    for copy in copies[7:]:
        copy.start()

    first_row, last_row = row_at == 0, row_at == rows_of - 1
    first_col, last_col = col_at == 0, col_at == cols_of - 1

    for b in range(2):
        for r in range(0, TALL, 4):
            x = xe[r : r + 4].reshape(4 * WIDE, CH)
            inr[r : r + 4] = jnp.maximum(mm(x, v_red[b]), 0.0).reshape(4, WIDE, INNER)
        inr[0:2] = jnp.where(first_row, 0.0, inr[0:2])
        inr[34:36] = jnp.where(last_row, 0.0, inr[34:36])
        inr[:, 40:48] = jnp.where(first_col, 0.0, inr[:, 40:48])
        inr[:, 32:40] = jnp.where(last_col, 0.0, inr[:, 32:40])

        for r in range(TALL):
            line = inr[r]
            cat[r, :, :INNER] = pltpu.roll(line, 1, 0).astype(BF)
            cat[r, :, INNER : 2 * INNER] = line.astype(BF)
            cat[r, :, 2 * INNER :] = pltpu.roll(line, WIDE - 1, 0).astype(BF)

        for r, per in ((1, 7), (8, 7), (15, 7), (22, 7), (29, 6)) if b == 0 else (
            (2, 8), (10, 8), (18, 8), (26, 8)
        ):
            width = WIDE if b == 0 else TILE
            lhs = jnp.concatenate(
                [cat[r + i - 1 : r + i - 1 + per, :width] for i in range(3)], axis=2
            )
            h = jnp.maximum(mm(lhs.reshape(per * width, 9 * INNER), v_spa[b]), 0.0).astype(BF)
            y = mm(h, v_exp[b]) + xe[r : r + per, :width].reshape(per * width, CH).astype(F32)
            y = jnp.maximum(y, 0.0).astype(BF).reshape(per, width, CH)
            if b == 0:
                xe[r : r + per] = y
            else:
                xs[1, r - 1 : r - 1 + per] = y
                flat = y.reshape(per * TILE, CH).astype(F32)
                for j, shift in ((0, 1), (2, per * TILE - 1)):
                    moved = pltpu.roll(flat, shift, 0).astype(BF)
                    xs[j, r - 1 : r - 1 + per] = moved.reshape(per, TILE, CH)

    out_copy = pltpu.make_async_copy(xs.at[1, 1 : TILE + 1], sec, sems.at[12])
    out_copy.start()
    copies[7].wait()
    copies[8].wait()

    def stem_rows(k, _):
        r = k * 8
        for i in range(3):
            for j in range(3):
                lhs = xs[j, pl.ds(r + i, 8)].reshape(8 * TILE, CH)
                prod[3 * i + j, : 8 * TILE] = mm(lhs, v_first[3 * i + j])
        sums = []
        for i in range(3):
            t0, t1, t2 = (prod[3 * i + j, : 8 * TILE] for j in range(3))
            right = t0 + t1
            sums.append((t1 + t2, right + t2, right))
        for cv in range(3):
            a0, a1, a2 = sums[0][cv], sums[1][cv], sums[2][cv]
            low = a0 + a1
            for rv, value in enumerate((a1 + a2, low + a2, low)):
                if (rv, k) in ((0, 3), (2, 0)):
                    continue
                value = jnp.maximum(value, 0.0).astype(BF).reshape(8, TILE, MASK_CH)
                mv[3 * rv + cv, pl.ds(r, 8)] = value
        red = mm(xs[1, pl.ds(r + 1, 8)].reshape(8 * TILE, CH), v_br[...])
        redf[pl.ds(pl.multiple_of(r * TILE, 8), 8 * TILE), :] = red
        return 0

    for k in range(4):
        stem_rows(k, 0)

    def average_rows(k, _):
        here = pl.multiple_of(k * 4 * TILE, 8)
        block = redf[pl.ds(here, 5 * TILE + 8), :]
        pair = block[: 5 * TILE] + block[1 : 5 * TILE + 1]
        quad = (pair[: 4 * TILE] + pair[TILE:]) * 0.25
        avg[pl.ds(k * 4, 4)] = quad.astype(BF).reshape(4, TILE, BOX_CH)
        return 0

    lax.fori_loop(0, 8, average_rows, 0, unroll=True)

    inside = CROP - 2

    def choose(picker, source):
        return mm(picker, source).astype(BF)

    def table(v, r):
        return mv[v, pl.ds(r, WINDOW)].reshape(SPAN, MASK_CH)

    last = CROP - 1
    half = CROP // 2

    def gather_inside(r, v):
        got = choose(pick[1:last].reshape(inside * SLOTS, SPAN), table(v, r))
        got = got.reshape(2, half - 1, SLOTS, MASK_CH)
        ma[r + 1, 1, 1:half] = got[0]
        ma[r + 1, 0, 1:half] = got[1]

    copies[9].wait()
    for r in range(1, last):
        gather_inside(r, 4)
        quarter = (r - 1) % 4 * (MASK_CH // 4)
        filter_weights(v_rest, v_fil, (r - 1) // 4, slice(quarter, quarter + MASK_CH // 4))
    for r, v in ((0, 1), (last, 7)):
        gather_inside(r, v)
        ma[r + 1, 1, 0] = choose(pick[0], table(v - 1, r))
        ma[r + 1, 0, half] = choose(pick[last], table(v + 1, r))
    for side, v in ((0, 3), (1, 5)):
        got = choose(
            pick_side[side].reshape(inside * SLOTS, TILE * TILE),
            mv[v, 0:TILE].reshape(TILE * TILE, MASK_CH),
        )
        ma[2:CROP, 1 - side, side * half] = got.reshape(inside, SLOTS, MASK_CH)

    for copy in copies[10:12]:
        copy.wait()

    def filtered(layer, source, group):
        tiles = []
        for t in group:
            d0, d1, d2, d3 = (source[2 * t + k] for k in range(4))
            tile = []
            for w in (d0 - d2, d1 + d2, d2 - d1, d1 - d3):
                even, odd = w[0], w[1]
                e0, e1, o0, o1 = even[:half], even[1:], odd[:half], odd[1:]
                tile += [e0 - e1, o0 + e1, e1 - o0, o0 - o1]
            tiles.append(tile)
        size = half * SLOTS
        for k in range(16):
            lhs = jnp.concatenate([tile[k].reshape(size, MASK_CH) for tile in tiles], axis=0)
            prod[k, : len(group) * size] = mm(lhs, v_fil[layer, k])
        for n, t in enumerate(group):
            lines = []
            for xi in range(4):
                m0, m1, m2, m3 = (
                    prod[4 * xi + nu, n * size : (n + 1) * size] for nu in range(4)
                )
                lines.append((m0 + m1 + m2, m1 - m2 - m3))
            for b in range(2):
                y0, y1, y2, y3 = (lines[xi][b] for xi in range(4))
                for a, y in enumerate((y0 + y1 + y2, y1 - y2 - y3)):
                    yield t, a, b, jnp.maximum(y, 0.0).astype(BF)

    cell_lane = lax.broadcasted_iota(jnp.int32, (SLOTS, 128), 1)
    logits = [jnp.zeros((SLOTS, 128), F32)] * 2
    total = jnp.zeros((SLOTS, FC), F32)
    even = pick[0:half].reshape(half * SLOTS, SPAN)

    for layer in range(3):
        source, target = (ma, mb) if layer % 2 == 0 else (mb, ma)
        for group in GROUPS:
            final = []
            for t, a, b, act in filtered(layer, source, group):
                if layer < 2:
                    act = act.reshape(half, SLOTS, MASK_CH)
                    target[2 * t + a + 1, 1 - b, b : b + half] = act
                    continue
                final.append(act)
                if len(final) < 4:
                    continue
                got = mm(jnp.concatenate(final, axis=0), log_w)
                final = []
                for k in range(4 * half):
                    u = k % half
                    b, a = divmod(k // half, 2)
                    h, cell = divmod((2 * t + a) * CROP + 2 * u + b, 128)
                    part = got[k * SLOTS : (k + 1) * SLOTS]
                    logits[h] = jnp.where(cell_lane == cell, part, logits[h])
            for t in group:
                if layer == 0:
                    got = choose(even, avg[2 * t : 2 * t + WINDOW].reshape(SPAN, BOX_CH))
                    for u in range(half):
                        part = got[u * SLOTS : (u + 1) * SLOTS]
                        box_t[t, :, u * BOX_CH : (u + 1) * BOX_CH] = part
                if layer == 1:
                    part = v_bh[t * half * BOX_CH : (t + 1) * half * BOX_CH, :]
                    total = total + mm(box_t[t], part)
    logits = jnp.where(used_column > 0, jnp.concatenate(logits, axis=1), 0.0)
    lg[0, 0] = logits[:, : CROP * CROP]

    first_box = jnp.maximum(total, 0.0).astype(BF)
    next_box = jnp.maximum(mm(first_box, v_bs[...]), 0.0).astype(BF)
    scores = lax.dot_general(
        w_bp[...], next_box, (((1,), (1,)), ((), ())), preferred_element_type=F32
    )
    scores = jnp.where(used, scores, 0.0)
    for k in range(5):
        sc[0, k] = scores[k : k + 1]
    out_copy.wait()


def exchange(features):
    rows, cols = lax.axis_size("ty"), lax.axis_size("tx")

    def send(part, down, right):
        pairs = [
            (r * cols + c, (r + down) % rows * cols + c + right)
            for r in range(rows)
            for c in range(cols)
            if 0 <= c + right < cols
        ]
        return lax.ppermute(part, ("ty", "tx"), pairs)

    left = send(features[:, -2:], 0, 1)
    right = send(features[:, :2], 0, -1)
    edge = jnp.pad(left, ((0, 0), (14, 0), (0, 0))) + jnp.pad(right, ((0, 0), (0, 14), (0, 0)))
    top = send(jnp.concatenate([features[-2:], edge[-2:]], axis=1), 1, 0)
    bottom = send(jnp.concatenate([features[:2], edge[:2]], axis=1), -1, 0)
    return top, bottom, edge


def on_device(
    features, block_reduce, block_spatial, block_expand, mask_first, mask_rest, mask_logit,
    box_reduce, box_hidden, box_second, box_predict, roi_anchor, roi_dest, roi_slot,
):
    top, bottom, edge = exchange(features)
    hbm = pl.BlockSpec(memory_space=pl.ANY)
    vmem = pl.BlockSpec(memory_space=pltpu.VMEM)
    sec, lg, sc = pl.pallas_call(
        tile_kernel,
        out_shape=(
            jax.ShapeDtypeStruct((TILE, TILE, CH), BF),
            jax.ShapeDtypeStruct((1, 1, SLOTS, CROP * CROP), F32),
            jax.ShapeDtypeStruct((1, 5, 1, SLOTS), F32),
        ),
        in_specs=[hbm] * 9 + [vmem] + [hbm] * 3 + [vmem, vmem, vmem],
        out_specs=(hbm, vmem, vmem),
        scratch_shapes=[
            pltpu.VMEM((TALL, WIDE, CH), BF),
            pltpu.VMEM((TALL, WIDE, INNER), F32),
            pltpu.VMEM((TALL, WIDE, 3 * INNER), BF),
            pltpu.VMEM((3, TILE + 2, TILE, CH), BF),
            pltpu.VMEM((9, TILE + 2, TILE, MASK_CH), BF),
            pltpu.VMEM((TILE * TILE + 40, BOX_CH), F32),
            pltpu.VMEM((TILE, TILE, BOX_CH), BF),
            pltpu.VMEM((CROP, SLOTS, SPAN), BF),
            pltpu.VMEM((2, CROP - 2, SLOTS, TILE * TILE), BF),
            pltpu.VMEM((16, 2, 8, SLOTS, MASK_CH), BF),
            pltpu.VMEM((16, 2, 8, SLOTS, MASK_CH), BF),
            pltpu.VMEM((16, 14 * SLOTS, MASK_CH), F32),
            pltpu.VMEM((CROP // 2, SLOTS, CROP // 2 * BOX_CH), BF),
            pltpu.VMEM((2, CH, INNER), BF),
            pltpu.VMEM((2, 9 * INNER, INNER), BF),
            pltpu.VMEM((2, INNER, CH), BF),
            pltpu.VMEM((9, CH, MASK_CH), BF),
            pltpu.VMEM((3, 9, MASK_CH, MASK_CH), BF),
            pltpu.VMEM((3, 16, MASK_CH, MASK_CH), BF),
            pltpu.VMEM((CH, BOX_CH), BF),
            pltpu.VMEM(((CROP // 2) ** 2 * BOX_CH, FC), BF),
            pltpu.VMEM((FC, FC), BF),
            pltpu.SemaphoreType.DMA((13,)),
        ],
        compiler_params=pltpu.CompilerParams(vmem_limit_bytes=62 * 1024 * 1024),
        name="tile_heads",
    )(
        features, top, bottom, edge,
        block_reduce, block_spatial.reshape(2, 9 * INNER, INNER), block_expand,
        mask_first, mask_rest, mask_logit,
        box_reduce, box_hidden, box_second, box_predict.T, roi_anchor[0, 0].T, roi_dest[0],
    )
    return sec, lg, sc.transpose(0, 2, 3, 1)


def solution(mesh):
    whole = P()
    in_specs = (P("ty", "tx", None),) + (whole,) * 10 + (
        P("ty", "tx", None, None), P("ty", "tx", None), P("ty", "tx", None),
    )
    out_specs = (P("ty", "tx", None), P("ty", "tx", None, None), P("ty", "tx", None, None))
    return jax.shard_map(
        on_device, mesh=mesh, in_specs=in_specs, out_specs=out_specs, check_vma=False
    )
```

```python
import jax
import jax.numpy as jnp
from jax import lax
from jax.experimental import pallas as pl
from jax.experimental.pallas import tpu as pltpu
from jax.sharding import PartitionSpec as P

CROP = 14
TILE = 32
WIDE = 48
TALL = 36
CH = 512
INNER = 128
MASK_CH = 256
BOX_CH = 128
FC = 1024
SLOTS = 32
WINDOW = 20
GROUPS = ((0, 1), (2, 3), (4, 5), (6,))
SPAN = WINDOW * TILE
BF = jnp.bfloat16
F32 = jnp.float32


def mm(a, b):
    return jnp.dot(a, b, preferred_element_type=F32)


def spread(a, b, c):
    even, odd = (a + c) * 0.5, b * 0.5
    return a, even + odd, even - odd, c


def filter_weights(w, u, layer, part):
    taps = [w[layer, k, part].astype(F32) for k in range(9)]
    rows = [spread(taps[j], taps[3 + j], taps[6 + j]) for j in range(3)]
    for xi in range(4):
        for nu, value in enumerate(spread(rows[0][xi], rows[1][xi], rows[2][xi])):
            u[layer, 4 * xi + nu, part] = value.astype(BF)


def tile_kernel(
    feat, top, bottom, edge, w_red, w_spa, w_exp, w_first, w_rest, w_log, w_br, w_bh, w_bs, w_bp,
    anchor, dest,
    sec, lg, sc,
    xe, inr, cat, xs, mv, redf, avg, pick, pick_side, ma, mb, prod, box_t,
    v_red, v_spa, v_exp, v_first, v_rest, v_fil, v_br, v_bh, v_bs,
    sems,
):
    row_at = lax.axis_index("ty")
    col_at = lax.axis_index("tx")
    rows_of = lax.axis_size("ty")
    cols_of = lax.axis_size("tx")

    copies = [
        pltpu.make_async_copy(feat, xe.at[2:34, 0:TILE], sems.at[0]),
        pltpu.make_async_copy(top, xe.at[0:2], sems.at[1]),
        pltpu.make_async_copy(bottom, xe.at[34:36], sems.at[2]),
        pltpu.make_async_copy(edge, xe.at[2:34, TILE:WIDE], sems.at[3]),
        pltpu.make_async_copy(w_red, v_red, sems.at[4]),
        pltpu.make_async_copy(w_spa, v_spa, sems.at[5]),
        pltpu.make_async_copy(w_exp, v_exp, sems.at[6]),
        pltpu.make_async_copy(w_first, v_first, sems.at[7]),
        pltpu.make_async_copy(w_br, v_br, sems.at[8]),
        pltpu.make_async_copy(w_rest, v_rest, sems.at[9]),
        pltpu.make_async_copy(w_bh, v_bh, sems.at[10]),
        pltpu.make_async_copy(w_bs, v_bs, sems.at[11]),
    ]
    for copy in copies[:7]:
        copy.start()

    for j in range(3):
        xs[j, 0, :, :] = jnp.zeros((TILE, CH), BF)
        xs[j, TILE + 1, :, :] = jnp.zeros((TILE, CH), BF)
    for v in range(9):
        mv[v, TILE : TILE + 2, :, :] = jnp.zeros((2, TILE, MASK_CH), BF)
    redf[TILE * TILE : TILE * TILE + 40, :] = jnp.zeros((40, BOX_CH), F32)
    line = jnp.zeros((8, SLOTS, MASK_CH), BF)
    for ref in (ma, mb):
        for parity in range(2):
            ref[0, parity] = line
            ref[15, parity] = line
        for r in range(1, 15):
            ref[r, 0, 0] = line[0]
            ref[r, 1, 7] = line[0]

    def column(row):
        return jnp.broadcast_to(row.astype(F32), (SLOTS, SLOTS)).T[:, :1].astype(jnp.int32)

    used = dest[...] >= 0
    used_column = column(used)
    at = column(anchor[0:1] * TILE + anchor[1:2])
    log_w = jnp.broadcast_to(w_log[...].reshape(1, MASK_CH).astype(F32), (128, MASK_CH)).T.astype(BF)
    lanes = lax.broadcasted_iota(jnp.int32, (SLOTS, SPAN), 1) - at
    for k, c in enumerate([*range(0, CROP, 2), *range(1, CROP, 2)]):
        pick[k] = jnp.where(lanes == c, 1.0, 0.0).astype(BF)
    lanes = lax.broadcasted_iota(jnp.int32, (SLOTS, TILE * TILE), 1) - at
    for side, c in enumerate((0, CROP - 1)):
        for r in range(1, CROP - 1):
            pick_side[side, r - 1] = jnp.where(lanes == r * TILE + c, 1.0, 0.0).astype(BF)

    for copy in copies[:5]:
        copy.wait()
    for copy in copies[7:]:
        copy.start()

    first_row, last_row = row_at == 0, row_at == rows_of - 1
    first_col, last_col = col_at == 0, col_at == cols_of - 1

    for b in range(2):
        for r in range(0, TALL, 4):
            x = xe[r : r + 4].reshape(4 * WIDE, CH)
            inr[r : r + 4] = jnp.maximum(mm(x, v_red[b]), 0.0).reshape(4, WIDE, INNER)
        inr[0:2] = jnp.where(first_row, 0.0, inr[0:2])
        inr[34:36] = jnp.where(last_row, 0.0, inr[34:36])
        inr[:, 40:48] = jnp.where(first_col, 0.0, inr[:, 40:48])
        inr[:, 32:40] = jnp.where(last_col, 0.0, inr[:, 32:40])

        if b == 0:
            copies[5].wait()
            copies[6].wait()
        for r in range(TALL):
            line = inr[r]
            cat[r, :, :INNER] = pltpu.roll(line, 1, 0).astype(BF)
            cat[r, :, INNER : 2 * INNER] = line.astype(BF)
            cat[r, :, 2 * INNER :] = pltpu.roll(line, WIDE - 1, 0).astype(BF)

        for r, per in ((1, 7), (8, 7), (15, 7), (22, 7), (29, 6)) if b == 0 else (
            (2, 8), (10, 8), (18, 8), (26, 8)
        ):
            width = WIDE if b == 0 else TILE
            lhs = jnp.concatenate(
                [cat[r + i - 1 : r + i - 1 + per, :width] for i in range(3)], axis=2
            )
            h = jnp.maximum(mm(lhs.reshape(per * width, 9 * INNER), v_spa[b]), 0.0).astype(BF)
            y = mm(h, v_exp[b]) + xe[r : r + per, :width].reshape(per * width, CH).astype(F32)
            y = jnp.maximum(y, 0.0).astype(BF).reshape(per, width, CH)
            if b == 0:
                xe[r : r + per] = y
            else:
                xs[1, r - 1 : r - 1 + per] = y
                flat = y.reshape(per * TILE, CH).astype(F32)
                for j, shift in ((0, 1), (2, per * TILE - 1)):
                    moved = pltpu.roll(flat, shift, 0).astype(BF)
                    xs[j, r - 1 : r - 1 + per] = moved.reshape(per, TILE, CH)

    out_copy = pltpu.make_async_copy(xs.at[1, 1 : TILE + 1], sec, sems.at[12])
    out_copy.start()
    copies[7].wait()
    copies[8].wait()

    def stem_rows(k, _):
        r = k * 8
        for i in range(3):
            for j in range(3):
                lhs = xs[j, pl.ds(r + i, 8)].reshape(8 * TILE, CH)
                prod[3 * i + j, : 8 * TILE] = mm(lhs, v_first[3 * i + j])
        sums = []
        for i in range(3):
            t0, t1, t2 = (prod[3 * i + j, : 8 * TILE] for j in range(3))
            right = t0 + t1
            sums.append((t1 + t2, right + t2, right))
        for cv in range(3):
            a0, a1, a2 = sums[0][cv], sums[1][cv], sums[2][cv]
            low = a0 + a1
            for rv, value in enumerate((a1 + a2, low + a2, low)):
                if (rv, k) in ((0, 3), (2, 0)):
                    continue
                value = jnp.maximum(value, 0.0).astype(BF).reshape(8, TILE, MASK_CH)
                mv[3 * rv + cv, pl.ds(r, 8)] = value
        red = mm(xs[1, pl.ds(r + 1, 8)].reshape(8 * TILE, CH), v_br[...])
        redf[pl.ds(pl.multiple_of(r * TILE, 8), 8 * TILE), :] = red
        return 0

    for k in range(4):
        stem_rows(k, 0)

    def average_rows(k, _):
        here = pl.multiple_of(k * 4 * TILE, 8)
        block = redf[pl.ds(here, 5 * TILE + 8), :]
        pair = block[: 5 * TILE] + block[1 : 5 * TILE + 1]
        quad = (pair[: 4 * TILE] + pair[TILE:]) * 0.25
        avg[pl.ds(k * 4, 4)] = quad.astype(BF).reshape(4, TILE, BOX_CH)
        return 0

    lax.fori_loop(0, 8, average_rows, 0, unroll=True)

    inside = CROP - 2

    def choose(picker, source):
        return mm(picker, source).astype(BF)

    def table(v, r):
        return mv[v, pl.ds(r, WINDOW)].reshape(SPAN, MASK_CH)

    last = CROP - 1
    half = CROP // 2

    def gather_inside(r, v):
        got = choose(pick[1:last].reshape(inside * SLOTS, SPAN), table(v, r))
        got = got.reshape(2, half - 1, SLOTS, MASK_CH)
        ma[r + 1, 1, 1:half] = got[0]
        ma[r + 1, 0, 1:half] = got[1]

    copies[9].wait()
    for r in range(1, last):
        gather_inside(r, 4)
        quarter = (r - 1) % 4 * (MASK_CH // 4)
        filter_weights(v_rest, v_fil, (r - 1) // 4, slice(quarter, quarter + MASK_CH // 4))
    for r, v in ((0, 1), (last, 7)):
        gather_inside(r, v)
        ma[r + 1, 1, 0] = choose(pick[0], table(v - 1, r))
        ma[r + 1, 0, half] = choose(pick[last], table(v + 1, r))
    for side, v in ((0, 3), (1, 5)):
        got = choose(
            pick_side[side].reshape(inside * SLOTS, TILE * TILE),
            mv[v, 0:TILE].reshape(TILE * TILE, MASK_CH),
        )
        ma[2:CROP, 1 - side, side * half] = got.reshape(inside, SLOTS, MASK_CH)

    for copy in copies[10:12]:
        copy.wait()

    def filtered(layer, source, group):
        tiles = []
        for t in group:
            d0, d1, d2, d3 = (source[2 * t + k] for k in range(4))
            tile = []
            for w in (d0 - d2, d1 + d2, d2 - d1, d1 - d3):
                even, odd = w[0], w[1]
                e0, e1, o0, o1 = even[:half], even[1:], odd[:half], odd[1:]
                tile += [e0 - e1, o0 + e1, e1 - o0, o0 - o1]
            tiles.append(tile)
        size = half * SLOTS
        for k in range(16):
            lhs = jnp.concatenate([tile[k].reshape(size, MASK_CH) for tile in tiles], axis=0)
            prod[k, : len(group) * size] = mm(lhs, v_fil[layer, k])
        for n, t in enumerate(group):
            lines = []
            for xi in range(4):
                m0, m1, m2, m3 = (
                    prod[4 * xi + nu, n * size : (n + 1) * size] for nu in range(4)
                )
                lines.append((m0 + m1 + m2, m1 - m2 - m3))
            for b in range(2):
                y0, y1, y2, y3 = (lines[xi][b] for xi in range(4))
                for a, y in enumerate((y0 + y1 + y2, y1 - y2 - y3)):
                    yield t, a, b, jnp.maximum(y, 0.0).astype(BF)

    cell_lane = lax.broadcasted_iota(jnp.int32, (SLOTS, 128), 1)
    logits = [jnp.zeros((SLOTS, 128), F32)] * 2
    total = jnp.zeros((SLOTS, FC), F32)
    even = pick[0:half].reshape(half * SLOTS, SPAN)

    for layer in range(3):
        source, target = (ma, mb) if layer % 2 == 0 else (mb, ma)
        for group in GROUPS:
            final = []
            for t, a, b, act in filtered(layer, source, group):
                if layer < 2:
                    act = act.reshape(half, SLOTS, MASK_CH)
                    target[2 * t + a + 1, 1 - b, b : b + half] = act
                    continue
                final.append(act)
                if len(final) < 4:
                    continue
                got = mm(jnp.concatenate(final, axis=0), log_w)
                final = []
                for k in range(4 * half):
                    u = k % half
                    b, a = divmod(k // half, 2)
                    h, cell = divmod((2 * t + a) * CROP + 2 * u + b, 128)
                    part = got[k * SLOTS : (k + 1) * SLOTS]
                    logits[h] = jnp.where(cell_lane == cell, part, logits[h])
            for t in group:
                if layer == 0:
                    got = choose(even, avg[2 * t : 2 * t + WINDOW].reshape(SPAN, BOX_CH))
                    for u in range(half):
                        part = got[u * SLOTS : (u + 1) * SLOTS]
                        box_t[t, :, u * BOX_CH : (u + 1) * BOX_CH] = part
                if layer == 1:
                    part = v_bh[t * half * BOX_CH : (t + 1) * half * BOX_CH, :]
                    total = total + mm(box_t[t], part)
    logits = jnp.where(used_column > 0, jnp.concatenate(logits, axis=1), 0.0)
    lg[0, 0] = logits[:, : CROP * CROP]

    first_box = jnp.maximum(total, 0.0).astype(BF)
    next_box = jnp.maximum(mm(first_box, v_bs[...]), 0.0).astype(BF)
    scores = lax.dot_general(
        w_bp[...], next_box, (((1,), (1,)), ((), ())), preferred_element_type=F32
    )
    scores = jnp.where(used, scores, 0.0)
    for k in range(5):
        sc[0, k] = scores[k : k + 1]
    out_copy.wait()


def exchange(features):
    rows, cols = lax.axis_size("ty"), lax.axis_size("tx")

    def send(part, down, right):
        pairs = [
            (r * cols + c, (r + down) % rows * cols + c + right)
            for r in range(rows)
            for c in range(cols)
            if 0 <= c + right < cols
        ]
        return lax.ppermute(part, ("ty", "tx"), pairs)

    left = send(features[:, -2:], 0, 1)
    right = send(features[:, :2], 0, -1)
    edge = jnp.pad(left, ((0, 0), (14, 0), (0, 0))) + jnp.pad(right, ((0, 0), (0, 14), (0, 0)))
    top = send(jnp.concatenate([features[-2:], edge[-2:]], axis=1), 1, 0)
    bottom = send(jnp.concatenate([features[:2], edge[:2]], axis=1), -1, 0)
    return top, bottom, edge


def on_device(
    features, block_reduce, block_spatial, block_expand, mask_first, mask_rest, mask_logit,
    box_reduce, box_hidden, box_second, box_predict, roi_anchor, roi_dest, roi_slot,
):
    top, bottom, edge = exchange(features)
    hbm = pl.BlockSpec(memory_space=pl.ANY)
    vmem = pl.BlockSpec(memory_space=pltpu.VMEM)
    sec, lg, sc = pl.pallas_call(
        tile_kernel,
        out_shape=(
            jax.ShapeDtypeStruct((TILE, TILE, CH), BF),
            jax.ShapeDtypeStruct((1, 1, SLOTS, CROP * CROP), F32),
            jax.ShapeDtypeStruct((1, 5, 1, SLOTS), F32),
        ),
        in_specs=[hbm] * 9 + [vmem] + [hbm] * 3 + [vmem, vmem, vmem],
        out_specs=(hbm, vmem, vmem),
        scratch_shapes=[
            pltpu.VMEM((TALL, WIDE, CH), BF),
            pltpu.VMEM((TALL, WIDE, INNER), F32),
            pltpu.VMEM((TALL, WIDE, 3 * INNER), BF),
            pltpu.VMEM((3, TILE + 2, TILE, CH), BF),
            pltpu.VMEM((9, TILE + 2, TILE, MASK_CH), BF),
            pltpu.VMEM((TILE * TILE + 40, BOX_CH), F32),
            pltpu.VMEM((TILE, TILE, BOX_CH), BF),
            pltpu.VMEM((CROP, SLOTS, SPAN), BF),
            pltpu.VMEM((2, CROP - 2, SLOTS, TILE * TILE), BF),
            pltpu.VMEM((16, 2, 8, SLOTS, MASK_CH), BF),
            pltpu.VMEM((16, 2, 8, SLOTS, MASK_CH), BF),
            pltpu.VMEM((16, 14 * SLOTS, MASK_CH), F32),
            pltpu.VMEM((CROP // 2, SLOTS, CROP // 2 * BOX_CH), BF),
            pltpu.VMEM((2, CH, INNER), BF),
            pltpu.VMEM((2, 9 * INNER, INNER), BF),
            pltpu.VMEM((2, INNER, CH), BF),
            pltpu.VMEM((9, CH, MASK_CH), BF),
            pltpu.VMEM((3, 9, MASK_CH, MASK_CH), BF),
            pltpu.VMEM((3, 16, MASK_CH, MASK_CH), BF),
            pltpu.VMEM((CH, BOX_CH), BF),
            pltpu.VMEM(((CROP // 2) ** 2 * BOX_CH, FC), BF),
            pltpu.VMEM((FC, FC), BF),
            pltpu.SemaphoreType.DMA((13,)),
        ],
        compiler_params=pltpu.CompilerParams(vmem_limit_bytes=62 * 1024 * 1024),
        name="tile_heads",
    )(
        features, top, bottom, edge,
        block_reduce, block_spatial.reshape(2, 9 * INNER, INNER), block_expand,
        mask_first, mask_rest, mask_logit,
        box_reduce, box_hidden, box_second, box_predict.T, roi_anchor[0, 0].T, roi_dest[0],
    )
    return sec, lg, sc.transpose(0, 2, 3, 1)


def solution(mesh):
    whole = P()
    in_specs = (P("ty", "tx", None),) + (whole,) * 10 + (
        P("ty", "tx", None, None), P("ty", "tx", None), P("ty", "tx", None),
    )
    out_specs = (P("ty", "tx", None), P("ty", "tx", None, None), P("ty", "tx", None, None))
    return jax.shard_map(
        on_device, mesh=mesh, in_specs=in_specs, out_specs=out_specs, check_vma=False
    )
```
